32 devices in a mesh: row: 16 (over z, y, x), col: 2 (over core).
Axes of the slice: x: 2, y: 2, z: 4, core: 2. Of those that a mesh axis runs over, the one named last changes fastest.
Arguments:
- vectors: float32 [16384, 512], P('row', 'col'), may hold values from -6 to 6
- reflectors: float32 [2, 16384, 128], P('col', 'row'), may hold values from -0.375 to 0.375
- tfactors: float32 [2, 64, 128, 128], P('col', 'row'), may hold values from -0.05 to 1, as said below
- plan: int32 [2], replicated, may hold values from 0 to 1, each once
Outputs:
- result: float32 [16384, 512], P('row', 'col')
The draws below stay inside these ranges and needn't reach their ends.
Inputs may be any that keep to these rules, and one draw needn't show every extreme that they name: `plan`: every stored group is applied exactly once. `tfactors`: each factor is upper triangular with diagonal between 0.2 and 1.
All inputs are finite; a program needn't handle non-finite values.
Results may differ from the reference program's by a relative error of at most 0.00019.
Values sent between devices are 32-bit elements; how exact they have to be, the bound alone decides.
No kernel may reach another device: no remote copies, remote signals or barrier semaphores. Data moves between devices by JAX's collectives and lax.ppermute only.
A program may use at most 64 MiB of HBM per device.

```python
import jax
import jax.numpy as jnp
from jax import lax

NB = 128
GROUPS = 2
M = 16384
E = 512


def draw_tfactors(key, part):
    first, second = jax.random.split(jax.random.fold_in(key, 7))
    shape = (GROUPS, M // (2 * NB), NB, NB)
    upper_part = jnp.clip(jax.random.normal(first, shape, jnp.float32) * 0.02, -0.05, 0.05)
    diag_part = jax.random.uniform(second, shape[:3], jnp.float32, 0.3, 0.9)
    rowsix = jnp.arange(NB)[:, None]
    colsix = jnp.arange(NB)[None, :]
    above = (rowsix < colsix).astype(jnp.float32)
    ident = (rowsix == colsix).astype(jnp.float32)
    return upper_part * above + diag_part[..., None] * ident


def shard_levels(stream_key, dims, pieces, smallest, high):
    loudness, own = 1.0, jax.random.fold_in(stream_key, 6)
    for axis_at, parts in pieces:
        draws = jnp.exp(jax.random.uniform(jax.random.fold_in(own, axis_at), (parts,), jnp.float32, smallest / len(pieces), high / len(pieces)))
        loudness = loudness * jnp.repeat(draws, dims[axis_at] // parts).reshape([-1 if axis == axis_at else 1 for axis in range(len(dims))])
    return loudness


def normal_values(key, extent, spread, reach, cuts=(), held_as=jnp.bfloat16):
    result = spread * jax.random.normal(key, extent, jnp.float32)
    if cuts:
        result = result * shard_levels(key, extent, cuts, -0.22, 0.18)
    return jnp.clip(result, -reach, reach).astype(held_as)


def setup_inputs(seed: int = 0) -> dict:
    arg_keys = jax.random.split(jax.random.key(seed), 5)
    return {
        "vectors": normal_values(arg_keys[0], (M, E), 1.0, 6.0, ((0, 16), (1, 2)), jnp.float32),
        "reflectors": normal_values(arg_keys[1], (GROUPS, M, NB), (2 * NB) ** -0.5, 0.375, ((0, 2), (1, 16)), jnp.float32),
        "tfactors": draw_tfactors(jax.random.fold_in(arg_keys[4], 71), 0),
        "plan": jax.random.permutation(arg_keys[3], GROUPS).astype(jnp.int32),
    }


def apply_blocks(vectors, block, factor):
    rows = 2 * NB
    count = vectors.shape[0] // rows
    shaped = vectors.reshape(count, rows, vectors.shape[1])
    refl = block.reshape(count, rows, NB)
    proj = jnp.einsum("kri,krc->kic", refl, shaped, precision=lax.Precision.HIGHEST)
    coeff = jnp.einsum("kij,kjc->kic", factor, proj, precision=lax.Precision.HIGHEST)
    update = jnp.einsum("kri,kic->krc", refl, coeff, precision=lax.Precision.HIGHEST)
    return (shaped - update).reshape(vectors.shape)


def reference(vectors, reflectors, tfactors, plan):
    total = M // (2 * NB)
    for step in range(GROUPS):
        chosen = plan[step].astype(jnp.int32)
        block = lax.dynamic_index_in_dim(reflectors, chosen, 0, False)
        factor = lax.dynamic_index_in_dim(tfactors, chosen, 0, False)
        if step % 2 == 0:
            vectors = apply_blocks(vectors, block, factor)
        else:
            middle = apply_blocks(vectors[NB:M - NB], block[NB:M - NB], factor[:total - 1])
            vectors = jnp.concatenate([vectors[:NB], middle, vectors[M - NB:]], axis=0)
    return vectors
```

```python
import jax
import jax.numpy as jnp
from jax import lax
from jax.experimental import pallas as pl
from jax.experimental.pallas import tpu as pltpu
from jax.sharding import PartitionSpec as P

F32 = jnp.float32
BF16 = jnp.bfloat16
VMEM = pl.BlockSpec(memory_space=pltpu.VMEM)
SMEM = pl.BlockSpec(memory_space=pltpu.SMEM)
ANY = pl.BlockSpec(memory_space=pl.ANY)


def split(a):
    high = a.astype(BF16)
    return high, (a - high.astype(F32)).astype(BF16)


def dot(a, b, over):
    return lax.dot_general(a, b, (((over,), (0,)), ((), ())), preferred_element_type=F32)


def product(a, b, over=1):
    (ah, al), (bh, bl) = a, b
    return dot(ah, bh, over) + (dot(ah, bl, over) + dot(al, bh, over))


def reflect(x, refl, factor):
    v = split(refl)
    coeff = product(split(factor), split(product(v, split(x), over=0)))
    return x - product(v, split(coeff))


def pick(kinds, step, pieces):
    value = pieces[0]
    for at, piece in enumerate(pieces[1:], 1):
        mask = jnp.broadcast_to(kinds[step : step + 1, :], value.shape) == at
        value = jnp.where(mask, piece, value)
    return value


def vmem_call(body, outs, specs, name, **rest):
    return pl.pallas_call(
        body,
        out_shape=outs,
        in_specs=specs,
        out_specs=[ANY if getattr(o, "far", False) else VMEM for o in outs],
        name=name,
        **rest,
    )


def shape(*dims, dtype=F32):
    return jax.ShapeDtypeStruct(dims, dtype)


def kinds_of(plan, columns, held, lanes):
    def body(plan_ref, out_ref):
        me = lax.axis_index("col")
        out_ref[...] = jnp.zeros_like(out_ref)
        for step in range(plan.shape[0]):
            group = plan_ref[step]
            home, slot = group // held, group % held
            piece = (me + columns - home) % columns * held + slot
            out_ref[step : step + 1, :] = jnp.full((1, lanes), piece, jnp.int32)

    rows = -(-plan.shape[0] // 8) * 8
    return vmem_call(body, [shape(rows, lanes, dtype=jnp.int32)], [SMEM], "kinds")(plan)[0]


def is_top(odd_round):
    return (lax.axis_index("row") % 2 == 1) != odd_round


def edge(x, refls, factors, kinds, step, odd_round):
    height, width = x.shape
    strip = refls[0].shape[1]
    count = height // (2 * strip)
    n = len(refls)

    def body(*refs):
        kinds_ref, x_ref, refs = refs[0], refs[1], refs[2:]
        refl_refs, factor_refs = refs[:n], refs[n : 2 * n]
        block_ref, proj_ref = refs[2 * n :]

        def work(at, outer):
            rows = pl.ds(at * 2 * strip, 2 * strip)
            side = pl.ds(at * 2 * strip + outer, strip)
            first = pick(kinds_ref, step, [r[rows, :] for r in refl_refs])
            factor = pick(kinds_ref, step, [r[at] for r in factor_refs])
            second = pick(kinds_ref, step + 1, [r[side, :] for r in refl_refs])
            new = reflect(x_ref[rows, :], first, factor)
            block_ref[...] = new
            proj_ref[...] = product(split(second), split(new[outer : outer + strip]), over=0)

        top = is_top(odd_round)
        pl.when(top)(lambda: work(0, 0))
        pl.when(jnp.logical_not(top))(lambda: work(count - 1, strip))

    return vmem_call(
        body,
        [shape(2 * strip, width), shape(strip, width)],
        [VMEM] * (2 + 2 * n),
        "edge",
    )(kinds, x, *refls, *factors)


def middle(x, refls, factors, kinds, step, even_block, odd_block):
    height, width = x.shape
    strip = refls[0].shape[1]
    count = height // (2 * strip)
    n = len(refls)

    def body(*refs):
        kinds_ref, x_ref, even_ref, odd_ref, refs = refs[0], refs[1], refs[2], refs[3], refs[4:]
        refl_refs, factor_refs = refs[:n], refs[n : 2 * n]
        out_ref, work_ref, sem = refs[2 * n :]
        top_even = is_top(False)
        head = jnp.where(top_even, even_ref[strip:, :], odd_ref[strip:, :])
        tail = jnp.where(top_even, odd_ref[:strip, :], even_ref[:strip, :])
        for at in range(1, count - 1):
            rows = pl.ds(at * 2 * strip, 2 * strip)
            refl = pick(kinds_ref, step, [r[rows, :] for r in refl_refs])
            factor = pick(kinds_ref, step, [r[at] for r in factor_refs])
            work_ref[rows, :] = reflect(x_ref[rows, :], refl, factor)
        work_ref[pl.ds(strip, strip), :] = head
        work_ref[pl.ds(height - 2 * strip, strip), :] = tail
        copies = []
        for at in range(count - 1):
            rows = pl.ds(at * 2 * strip + strip, 2 * strip)
            refl = pick(kinds_ref, step + 1, [r[rows, :] for r in refl_refs])
            factor = pick(kinds_ref, step + 1, [r[at] for r in factor_refs])
            work_ref[rows, :] = reflect(work_ref[rows, :], refl, factor)
            copy = pltpu.make_async_copy(work_ref.at[rows, :], out_ref.at[rows, :], sem.at[at])
            copy.start()
            copies.append(copy)
        for copy in copies:
            copy.wait()

    return pl.pallas_call(
        body,
        out_shape=shape(height, width),
        in_specs=[VMEM] * (4 + 2 * n),
        out_specs=ANY,
        scratch_shapes=[pltpu.VMEM((height, width), F32), pltpu.SemaphoreType.DMA((count - 1,))],
        name="middle",
    )(kinds, x, even_block, odd_block, *refls, *factors)


def prepare(refls, factors, behind, kinds, step, odd_round, block, proj):
    height, strip = refls[0].shape
    width = block.shape[1]
    count = height // (2 * strip)
    n = len(refls)

    def body(*refs):
        kinds_ref, block_ref, proj_ref, refs = refs[0], refs[1], refs[2], refs[3:]
        refl_refs, factor_refs, behind_refs = refs[:n], refs[n : 2 * n], refs[2 * n : 3 * n]
        rest_ref, high_ref, low_ref = refs[3 * n :]
        row, last = lax.axis_index("row"), lax.axis_size("row") - 1

        def work(start, outer, factor, present):
            refl = pick(kinds_ref, step + 1, [r[pl.ds(start, strip), :] for r in refl_refs])
            weight = product(split(refl), split(factor))
            weight = jnp.where(present, weight, jnp.zeros_like(weight))
            high, low = split(weight)
            high_ref[...] = high
            low_ref[...] = low
            own = product((high, low), split(proj_ref[...]))
            rest_ref[...] = block_ref[outer : outer + strip, :] - own

        top = is_top(odd_round)

        @pl.when(top)
        def _():
            work(0, 0, pick(kinds_ref, step + 1, [r[...] for r in behind_refs]), row > 0)

        @pl.when(jnp.logical_not(top))
        def _():
            factor = pick(kinds_ref, step + 1, [r[count - 1] for r in factor_refs])
            work(height - strip, strip, factor, row < last)

    return vmem_call(
        body,
        [shape(strip, width), shape(strip, strip, dtype=BF16), shape(strip, strip, dtype=BF16)],
        [VMEM] * (3 + 3 * n),
        "prepare",
    )(kinds, block, proj, *refls, *factors, *behind)


def finish(out, odd_round, rest, high, low, got):
    height, width = out.shape
    strip = rest.shape[0]

    def body(rest_ref, high_ref, low_ref, got_ref, _, out_ref, new_ref, sem):
        row, last = lax.axis_index("row"), lax.axis_size("row") - 1
        top = is_top(odd_round)
        present = jnp.where(top, row > 0, row < last)
        other = jnp.where(present, got_ref[...], jnp.zeros_like(got_ref))
        new_ref[...] = rest_ref[...] - product((high_ref[...], low_ref[...]), split(other))
        start = pl.multiple_of(jnp.where(top, 0, height - strip), strip)
        copy = pltpu.make_async_copy(new_ref, out_ref.at[pl.ds(start, strip), :], sem)
        copy.start()
        copy.wait()

    return pl.pallas_call(
        body,
        out_shape=shape(height, width),
        in_specs=[VMEM] * 4 + [ANY],
        out_specs=ANY,
        scratch_shapes=[pltpu.VMEM((strip, width), F32), pltpu.SemaphoreType.DMA],
        input_output_aliases={4: 0},
        name="finish",
    )(rest, high, low, got, out)


def local(vectors, reflectors, tfactors, plan):
    groups = plan.shape[0]
    held, height, strip = reflectors.shape
    rows, columns = lax.axis_size("row"), lax.axis_size("col")

    def around(block, shift):
        return lax.ppermute(block, "col", [(c, (c + shift) % columns) for c in range(columns)])

    def trade(block, odd_round):
        route = []
        for row in range(rows):
            for col in range(columns):
                there = row + 1 if (row % 2 == 1) == odd_round else row - 1
                there = (there, col) if 0 <= there < rows else (row, (col + 1) % columns)
                route.append((row * columns + col, there[0] * columns + there[1]))
        return lax.ppermute(block, ("row", "col"), route)

    def everyone(piece):
        return [piece] + [around(piece, shift) for shift in range(1, columns)]

    def apart(pieces):
        return [piece[slot] for piece in pieces for slot in range(held)]

    refls = apart(everyone(reflectors))
    factors = apart(everyone(tfactors))
    behind = lax.ppermute(tfactors[:, -1], "row", [(r, (r + 1) % rows) for r in range(rows)])
    behinds = apart(everyone(behind))
    kinds = kinds_of(plan, columns, held, strip)
    current = vectors
    for step in range(0, groups, 2):
        even_block, even_proj = edge(current, refls, factors, kinds, step, False)
        even_got = trade(even_proj, False)
        odd_block, odd_proj = edge(current, refls, factors, kinds, step, True)
        odd_got = trade(odd_proj, True)
        done = middle(current, refls, factors, kinds, step, even_block, odd_block)
        even = prepare(refls, factors, behinds, kinds, step, False, even_block, even_proj)
        odd = prepare(refls, factors, behinds, kinds, step, True, odd_block, odd_proj)
        done = finish(done, False, *even, even_got)
        current = finish(done, True, *odd, odd_got)
    return current


def solution(mesh):
    return jax.shard_map(
        local,
        mesh=mesh,
        in_specs=(P("row", "col"), P("col", "row", None), P("col", "row", None, None), P()),
        out_specs=P("row", "col"),
        check_vma=False,
    )
```

```python
import jax
import jax.numpy as jnp
from jax import lax
from jax.experimental import pallas as pl
from jax.experimental.pallas import tpu as pltpu
from jax.sharding import PartitionSpec as P

F32 = jnp.float32
BF16 = jnp.bfloat16
VMEM = pl.BlockSpec(memory_space=pltpu.VMEM)
SMEM = pl.BlockSpec(memory_space=pltpu.SMEM)
ANY = pl.BlockSpec(memory_space=pl.ANY)
LEAN = pltpu.CompilerParams(vmem_limit_bytes=8 << 20)


def split(a):
    high = a.astype(BF16)
    return high, (a - high.astype(F32)).astype(BF16)


def dot(a, b, over):
    return lax.dot_general(a, b, (((over,), (0,)), ((), ())), preferred_element_type=F32)


def product(a, b, over=1):
    (ah, al), (bh, bl) = a, b
    return dot(ah, bh, over) + (dot(ah, bl, over) + dot(al, bh, over))


def reflect(x, refl, factor):
    v = split(refl)
    coeff = product(split(factor), split(product(v, split(x), over=0)))
    return x - product(v, split(coeff))


def pick(kinds, step, pieces):
    value = pieces[0]
    for at, piece in enumerate(pieces[1:], 1):
        mask = jnp.broadcast_to(kinds[step : step + 1, :], value.shape) == at
        value = jnp.where(mask, piece, value)
    return value


def vmem_call(body, outs, specs, name, **rest):
    return pl.pallas_call(
        body,
        out_shape=outs,
        in_specs=specs,
        out_specs=[VMEM] * len(outs),
        name=name,
        compiler_params=LEAN,
        **rest,
    )


def shape(*dims, dtype=F32):
    return pltpu.VMEM(dims, dtype)


def near(*values):
    return [pltpu.with_memory_space_constraint(value, pltpu.VMEM) for value in values]


def kinds_of(plan, columns, held, lanes):
    def body(plan_ref, out_ref):
        me = lax.axis_index("col")
        out_ref[...] = jnp.zeros_like(out_ref)
        for step in range(plan.shape[0]):
            group = plan_ref[step]
            home, slot = group // held, group % held
            piece = (me + columns - home) % columns * held + slot
            out_ref[step : step + 1, :] = jnp.full((1, lanes), piece, jnp.int32)

    rows = -(-plan.shape[0] // 8) * 8
    return vmem_call(body, [shape(rows, lanes, dtype=jnp.int32)], [SMEM], "kinds")(plan)[0]


def is_top(odd_round):
    return (lax.axis_index("row") % 2 == 1) != odd_round


def edge(x, refls, factors, kinds, step, odd_round):
    height, width = x.shape
    strip = refls[0].shape[1]
    count = height // (2 * strip)
    n = len(refls)

    def body(*refs):
        kinds_ref, x_ref, refs = refs[0], refs[1], refs[2:]
        refl_refs, factor_refs = refs[:n], refs[n : 2 * n]
        block_ref, proj_ref = refs[2 * n :]

        def work(at, outer):
            rows = pl.ds(at * 2 * strip, 2 * strip)
            side = pl.ds(at * 2 * strip + outer, strip)
            first = pick(kinds_ref, step, [r[rows, :] for r in refl_refs])
            factor = pick(kinds_ref, step, [r[at] for r in factor_refs])
            second = pick(kinds_ref, step + 1, [r[side, :] for r in refl_refs])
            new = reflect(x_ref[rows, :], first, factor)
            block_ref[...] = new
            proj_ref[...] = product(split(second), split(new[outer : outer + strip]), over=0)

        top = is_top(odd_round)
        pl.when(top)(lambda: work(0, 0))
        pl.when(jnp.logical_not(top))(lambda: work(count - 1, strip))

    return vmem_call(
        body,
        [shape(2 * strip, width), shape(strip, width)],
        [VMEM] * (2 + 2 * n),
        "edge",
    )(*near(kinds, x, *refls, *factors))


def middle(x, refls, factors, kinds, step, even_block, odd_block):
    height, width = x.shape
    strip = refls[0].shape[1]
    count = height // (2 * strip)
    n = len(refls)

    def body(*refs):
        kinds_ref, x_ref, even_ref, odd_ref, refs = refs[0], refs[1], refs[2], refs[3], refs[4:]
        refl_refs, factor_refs = refs[:n], refs[n : 2 * n]
        out_ref, work_ref, sem = refs[2 * n :]
        top_even = is_top(False)
        head = jnp.where(top_even, even_ref[strip:, :], odd_ref[strip:, :])
        tail = jnp.where(top_even, odd_ref[:strip, :], even_ref[:strip, :])
        for at in range(1, count - 1):
            rows = pl.ds(at * 2 * strip, 2 * strip)
            refl = pick(kinds_ref, step, [r[rows, :] for r in refl_refs])
            factor = pick(kinds_ref, step, [r[at] for r in factor_refs])
            work_ref[rows, :] = reflect(x_ref[rows, :], refl, factor)
        work_ref[pl.ds(strip, strip), :] = head
        work_ref[pl.ds(height - 2 * strip, strip), :] = tail
        copies = []
        for at in range(count - 1):
            rows = pl.ds(at * 2 * strip + strip, 2 * strip)
            refl = pick(kinds_ref, step + 1, [r[rows, :] for r in refl_refs])
            factor = pick(kinds_ref, step + 1, [r[at] for r in factor_refs])
            work_ref[rows, :] = reflect(work_ref[rows, :], refl, factor)
            copy = pltpu.make_async_copy(work_ref.at[rows, :], out_ref.at[rows, :], sem.at[at])
            copy.start()
            copies.append(copy)
        for copy in copies:
            copy.wait()

    return pl.pallas_call(
        body,
        out_shape=jax.ShapeDtypeStruct((height, width), F32),
        in_specs=[VMEM] * (4 + 2 * n),
        out_specs=ANY,
        scratch_shapes=[pltpu.VMEM((height, width), F32), pltpu.SemaphoreType.DMA((count - 1,))],
        name="middle",
        compiler_params=LEAN,
    )(*near(kinds, x, even_block, odd_block, *refls, *factors))


def prepare(refls, factors, behind, kinds, step, odd_round, block, proj):
    height, strip = refls[0].shape
    width = block.shape[1]
    count = height // (2 * strip)
    n = len(refls)

    def body(*refs):
        kinds_ref, block_ref, proj_ref, refs = refs[0], refs[1], refs[2], refs[3:]
        refl_refs, factor_refs, behind_refs = refs[:n], refs[n : 2 * n], refs[2 * n : 3 * n]
        rest_ref, high_ref, low_ref = refs[3 * n :]
        row, last = lax.axis_index("row"), lax.axis_size("row") - 1

        def work(start, outer, factor, present):
            refl = pick(kinds_ref, step + 1, [r[pl.ds(start, strip), :] for r in refl_refs])
            weight = product(split(refl), split(factor))
            weight = jnp.where(present, weight, jnp.zeros_like(weight))
            high, low = split(weight)
            high_ref[...] = high
            low_ref[...] = low
            own = product((high, low), split(proj_ref[...]))
            rest_ref[...] = block_ref[outer : outer + strip, :] - own

        top = is_top(odd_round)

        @pl.when(top)
        def _():
            work(0, 0, pick(kinds_ref, step + 1, [r[...] for r in behind_refs]), row > 0)

        @pl.when(jnp.logical_not(top))
        def _():
            factor = pick(kinds_ref, step + 1, [r[count - 1] for r in factor_refs])
            work(height - strip, strip, factor, row < last)

    return vmem_call(
        body,
        [shape(strip, width), shape(strip, strip, dtype=BF16), shape(strip, strip, dtype=BF16)],
        [VMEM] * (3 + 3 * n),
        "prepare",
    )(*near(kinds, block, proj, *refls, *factors, *behind))


def finish(out, odd_round, rest, high, low, got):
    height, width = out.shape
    strip = rest.shape[0]

    def body(rest_ref, high_ref, low_ref, got_ref, _, out_ref, new_ref, sem):
        row, last = lax.axis_index("row"), lax.axis_size("row") - 1
        top = is_top(odd_round)
        present = jnp.where(top, row > 0, row < last)
        other = jnp.where(present, got_ref[...], jnp.zeros_like(got_ref))
        new_ref[...] = rest_ref[...] - product((high_ref[...], low_ref[...]), split(other))
        start = pl.multiple_of(jnp.where(top, 0, height - strip), strip)
        copy = pltpu.make_async_copy(new_ref, out_ref.at[pl.ds(start, strip), :], sem)
        copy.start()
        copy.wait()

    return pl.pallas_call(
        body,
        out_shape=jax.ShapeDtypeStruct((height, width), F32),
        in_specs=[VMEM] * 4 + [ANY],
        out_specs=ANY,
        scratch_shapes=[pltpu.VMEM((strip, width), F32), pltpu.SemaphoreType.DMA],
        input_output_aliases={4: 0},
        name="finish",
        compiler_params=LEAN,
    )(*near(rest, high, low, got), out)


def local(vectors, reflectors, tfactors, plan):
    groups = plan.shape[0]
    held, height, strip = reflectors.shape
    rows, columns = lax.axis_size("row"), lax.axis_size("col")

    def around(block, shift):
        return lax.ppermute(block, "col", [(c, (c + shift) % columns) for c in range(columns)])

    def trade(block, odd_round):
        route = []
        for row in range(rows):
            for col in range(columns):
                there = row + 1 if (row % 2 == 1) == odd_round else row - 1
                there = (there, col) if 0 <= there < rows else (row, (col + 1) % columns)
                route.append((row * columns + col, there[0] * columns + there[1]))
        return lax.ppermute(block, ("row", "col"), route)

    def everyone(piece):
        return [piece] + [around(piece, shift) for shift in range(1, columns)]

    def apart(pieces):
        return [piece[slot] for piece in pieces for slot in range(held)]

    refls = apart(everyone(reflectors))
    factors = apart(everyone(tfactors))
    behind = lax.ppermute(tfactors[:, -1], "row", [(r, (r + 1) % rows) for r in range(rows)])
    behinds = apart(everyone(behind))
    kinds = kinds_of(plan, columns, held, strip)
    current = vectors
    for step in range(0, groups, 2):
        even_block, even_proj = edge(current, refls, factors, kinds, step, False)
        even_got = trade(even_proj, False)
        odd_block, odd_proj = edge(current, refls, factors, kinds, step, True)
        odd_got = trade(odd_proj, True)
        done = middle(current, refls, factors, kinds, step, even_block, odd_block)
        even = prepare(refls, factors, behinds, kinds, step, False, even_block, even_proj)
        odd = prepare(refls, factors, behinds, kinds, step, True, odd_block, odd_proj)
        done = finish(done, False, *even, even_got)
        current = finish(done, True, *odd, odd_got)
    return current


def solution(mesh):
    return jax.shard_map(
        local,
        mesh=mesh,
        in_specs=(P("row", "col"), P("col", "row", None), P("col", "row", None, None), P()),
        out_specs=P("row", "col"),
        check_vma=False,
    )
```

```python
import jax
import jax.numpy as jnp
from jax import lax
from jax.experimental import pallas as pl
from jax.experimental.pallas import tpu as pltpu
from jax.sharding import PartitionSpec as P

F32 = jnp.float32
BF16 = jnp.bfloat16
VMEM = pl.BlockSpec(memory_space=pltpu.VMEM)
HBM = pl.BlockSpec(memory_space=pltpu.HBM)
ANY = pl.BlockSpec(memory_space=pl.ANY)
LEAN = pltpu.CompilerParams(vmem_limit_bytes=8 << 20)


def split(a):
    high = a.astype(BF16)
    return high, (a - high.astype(F32)).astype(BF16)


def dot(a, b, over):
    return lax.dot_general(a, b, (((over,), (0,)), ((), ())), preferred_element_type=F32)


def product(a, b, over=1):
    (ah, al), (bh, bl) = a, b
    return dot(ah, bh, over) + (dot(ah, bl, over) + dot(al, bh, over))


def reflect(x, refl, factor):
    v = split(refl)
    coeff = product(split(factor), split(product(v, split(x), over=0)))
    return x - product(v, split(coeff))


def pick(kinds, step, pieces):
    value = pieces[0]
    for at, piece in enumerate(pieces[1:], 1):
        mask = jnp.broadcast_to(kinds[step : step + 1, :], value.shape) == at
        value = jnp.where(mask, piece, value)
    return value


def shape(*dims, dtype=F32):
    return pltpu.VMEM(dims, dtype)


def near(*values, space=pltpu.VMEM):
    return [pltpu.with_memory_space_constraint(value, space) for value in values]


def vmem_call(body, outs, name, *args):
    return pl.pallas_call(
        body,
        out_shape=outs,
        in_specs=[VMEM] * len(args),
        out_specs=[VMEM] * len(outs),
        name=name,
        compiler_params=LEAN,
    )(*near(*args))


def load(vectors, reflectors, tfactors, plan, columns):
    held, lanes = reflectors.shape[0], reflectors.shape[2]
    last = tfactors.shape[1] - 1
    groups = plan.shape[0]

    def body(plan, x, v, f, kinds_ref, x_out, v_out, f_out, end_out, plan_ref, sem):
        copies = [(plan, plan_ref), (f.at[:, last], end_out), (x, x_out), (v, v_out), (f, f_out)]
        copies = [pltpu.make_async_copy(*pair, sem.at[at]) for at, pair in enumerate(copies)]
        for copy in copies:
            copy.start()
        me = lax.axis_index("col")
        kinds_ref[...] = jnp.zeros_like(kinds_ref)
        copies[0].wait()
        for step in range(groups):
            group = plan_ref[step]
            piece = (me + columns - group // held) % columns * held + group % held
            kinds_ref[step : step + 1, :] = jnp.full((1, lanes), piece, jnp.int32)
        for copy in copies[1:]:
            copy.wait()

    return pl.pallas_call(
        body,
        out_shape=[
            shape(-(-groups // 8) * 8, lanes, dtype=jnp.int32),
            shape(*vectors.shape),
            shape(*reflectors.shape),
            shape(*tfactors.shape),
            shape(held, lanes, lanes),
        ],
        in_specs=[HBM] * 4,
        out_specs=[VMEM] * 5,
        scratch_shapes=[pltpu.SMEM((groups,), jnp.int32), pltpu.SemaphoreType.DMA((5,))],
        name="load",
        compiler_params=LEAN,
    )(*near(plan, vectors, reflectors, tfactors, space=pltpu.HBM))


def is_top(odd_round):
    return (lax.axis_index("row") % 2 == 1) != odd_round


def ordered(top, low):
    first = is_top(False)
    return jnp.where(first, top, low), jnp.where(first, low, top)


def edges(x, refls, factors, kinds, step):
    height, width = x.shape
    strip = refls[0].shape[1]
    count = height // (2 * strip)
    n = len(refls)

    def body(*refs):
        kinds_ref, x_ref, refs = refs[0], refs[1], refs[2:]
        refl_refs, factor_refs = refs[:n], refs[n : 2 * n]
        blocks, even_ref, odd_ref = refs[2 * n : 2 * n + 2], refs[2 * n + 2], refs[2 * n + 3]
        projs = []
        for at, outer, block_ref in zip((0, count - 1), (0, strip), blocks):
            rows = slice(at * 2 * strip, (at + 1) * 2 * strip)
            side = slice(rows.start + outer, rows.start + outer + strip)
            first = pick(kinds_ref, step, [r[rows, :] for r in refl_refs])
            factor = pick(kinds_ref, step, [r[at] for r in factor_refs])
            second = pick(kinds_ref, step + 1, [r[side, :] for r in refl_refs])
            new = reflect(x_ref[rows, :], first, factor)
            block_ref[...] = new
            projs.append(product(split(second), split(new[outer : outer + strip]), over=0))
        even_ref[...], odd_ref[...] = ordered(*projs)

    block, proj = shape(2 * strip, width), shape(strip, width)
    return vmem_call(body, [block, block, proj, proj], "edges", kinds, x, *refls, *factors)


def middle(x, refls, factors, kinds, step, top_block, low_block):
    height, width = x.shape
    strip = refls[0].shape[1]
    count = height // (2 * strip)
    n = len(refls)

    def body(*refs):
        kinds_ref, x_ref, top_ref, low_ref, refs = refs[0], refs[1], refs[2], refs[3], refs[4:]
        refl_refs, factor_refs = refs[:n], refs[n : 2 * n]
        out_ref, mark_ref, work_ref, sem = refs[2 * n :]
        mark_ref[...] = jnp.zeros_like(mark_ref)
        for at in range(1, count - 1):
            rows = pl.ds(at * 2 * strip, 2 * strip)
            refl = pick(kinds_ref, step, [r[rows, :] for r in refl_refs])
            factor = pick(kinds_ref, step, [r[at] for r in factor_refs])
            work_ref[rows, :] = reflect(x_ref[rows, :], refl, factor)
        work_ref[pl.ds(strip, strip), :] = top_ref[strip:, :]
        work_ref[pl.ds(height - 2 * strip, strip), :] = low_ref[:strip, :]
        copies = []
        for at in range(count - 1):
            rows = pl.ds(at * 2 * strip + strip, 2 * strip)
            refl = pick(kinds_ref, step + 1, [r[rows, :] for r in refl_refs])
            factor = pick(kinds_ref, step + 1, [r[at] for r in factor_refs])
            work_ref[rows, :] = reflect(work_ref[rows, :], refl, factor)
            copy = pltpu.make_async_copy(work_ref.at[rows, :], out_ref.at[rows, :], sem.at[at])
            copy.start()
            copies.append(copy)
        for copy in copies:
            copy.wait()

    args = near(kinds, x, top_block, low_block, *refls, *factors)
    return pl.pallas_call(
        body,
        out_shape=[jax.ShapeDtypeStruct((height, width), F32), shape(8, strip)],
        in_specs=[VMEM] * len(args),
        out_specs=[ANY, VMEM],
        scratch_shapes=[pltpu.VMEM((height, width), F32), pltpu.SemaphoreType.DMA((count - 1,))],
        name="middle",
        compiler_params=LEAN,
    )(*args)


def prepare(refls, factors, behind, kinds, step, blocks, projs, mark):
    height, strip = refls[0].shape
    width = blocks[0].shape[1]
    count = height // (2 * strip)
    n = len(refls)

    def body(_, kinds_ref, top_ref, low_ref, even_ref, odd_ref, *refs):
        refl_refs, factor_refs, behind_refs = refs[:n], refs[n : 2 * n], refs[2 * n : 3 * n]
        rests, highs, lows = refs[3 * n : 3 * n + 2], refs[3 * n + 2 : 3 * n + 4], refs[3 * n + 4 :]
        row, last = lax.axis_index("row"), lax.axis_size("row") - 1
        ends = [r[count - 1] for r in factor_refs], [r[...] for r in behind_refs]
        own = ordered(even_ref[...], odd_ref[...])

        def work(start, ends, present, strip_rows, proj):
            refl = pick(kinds_ref, step + 1, [r[start : start + strip, :] for r in refl_refs])
            weight = product(split(refl), split(pick(kinds_ref, step + 1, ends)))
            weight = jnp.where(present, weight, jnp.zeros_like(weight))
            parts = split(weight)
            return strip_rows - product(parts, split(proj)), *parts

        top = work(0, ends[1], row > 0, top_ref[:strip, :], own[0])
        low = work(height - strip, ends[0], row < last, low_ref[strip:, :], own[1])
        rests[0][...], rests[1][...] = ordered(top[0], low[0])
        for at, halves in ((1, highs), (2, lows)):
            even, odd = ordered(top[at].astype(F32), low[at].astype(F32))
            halves[0][...], halves[1][...] = even.astype(BF16), odd.astype(BF16)

    rest, half = shape(strip, width), shape(strip, strip, dtype=BF16)
    outs = vmem_call(
        body,
        [rest, rest, half, half, half, half],
        "prepare",
        *(mark, kinds, *blocks, *projs, *refls, *factors, *behind),
    )
    return outs[::2], outs[1::2]


def finish(out, odd_round, rest, high, low, got):
    height, width = out.shape
    strip = rest.shape[0]

    def body(rest_ref, high_ref, low_ref, got_ref, _, out_ref, new_ref, sem):
        row, last = lax.axis_index("row"), lax.axis_size("row") - 1
        top = is_top(odd_round)
        present = jnp.where(top, row > 0, row < last)
        other = jnp.where(present, got_ref[...], jnp.zeros_like(got_ref))
        new_ref[...] = rest_ref[...] - product((high_ref[...], low_ref[...]), split(other))
        start = pl.multiple_of(jnp.where(top, 0, height - strip), strip)
        copy = pltpu.make_async_copy(new_ref, out_ref.at[pl.ds(start, strip), :], sem)
        copy.start()
        copy.wait()

    return pl.pallas_call(
        body,
        out_shape=jax.ShapeDtypeStruct((height, width), F32),
        in_specs=[VMEM] * 4 + [ANY],
        out_specs=ANY,
        scratch_shapes=[pltpu.VMEM((strip, width), F32), pltpu.SemaphoreType.DMA],
        input_output_aliases={4: 0},
        name="finish",
        compiler_params=LEAN,
    )(*near(rest, high, low, got), out)


def local(vectors, reflectors, tfactors, plan):
    groups = plan.shape[0]
    held = reflectors.shape[0]
    rows, columns = lax.axis_size("row"), lax.axis_size("col")

    def around(block, shift):
        return lax.ppermute(block, "col", [(c, (c + shift) % columns) for c in range(columns)])

    def trade(block, odd_round):
        route = []
        for row in range(rows):
            for col in range(columns):
                there = row + 1 if (row % 2 == 1) == odd_round else row - 1
                there = (there, col) if 0 <= there < rows else (row, (col + 1) % columns)
                route.append((row * columns + col, there[0] * columns + there[1]))
        return lax.ppermute(block, ("row", "col"), route)

    def others(piece):
        return [around(piece, shift) for shift in range(1, columns)]

    def apart(pieces):
        return [piece[slot] for piece in pieces for slot in range(held)]

    far_refls, far_factors = others(reflectors), others(tfactors)
    kinds, current, refl, factor, end = load(vectors, reflectors, tfactors, plan, columns)
    behind = lax.ppermute(end, "row", [(r, (r + 1) % rows) for r in range(rows)])
    refls, factors = apart([refl, *far_refls]), apart([factor, *far_factors])
    behinds = apart([behind, *others(behind)])
    for step in range(0, groups, 2):
        top, low, even_proj, odd_proj = edges(current, refls, factors, kinds, step)
        even_got, odd_got = trade(even_proj, False), trade(odd_proj, True)
        done, mark = middle(current, refls, factors, kinds, step, top, low)
        even, odd = prepare(
            refls, factors, behinds, kinds, step, (top, low), (even_proj, odd_proj), mark
        )
        done = finish(done, False, *even, even_got)
        current = finish(done, True, *odd, odd_got)
    return current


def solution(mesh):
    return jax.shard_map(
        local,
        mesh=mesh,
        in_specs=(P("row", "col"), P("col", "row", None), P("col", "row", None, None), P()),
        out_specs=P("row", "col"),
        check_vma=False,
    )
```

```python
import jax
import jax.numpy as jnp
from jax import lax
from jax.experimental import pallas as pl
from jax.experimental.pallas import tpu as pltpu
from jax.sharding import PartitionSpec as P

F32 = jnp.float32
BF16 = jnp.bfloat16
LANES = 128
VMEM = pl.BlockSpec(memory_space=pltpu.VMEM)
HBM = pl.BlockSpec(memory_space=pltpu.HBM)
ANY = pl.BlockSpec(memory_space=pl.ANY)
LEAN = pltpu.CompilerParams(vmem_limit_bytes=8 << 20)


def split(a):
    high = a.astype(BF16)
    return high, (a - high.astype(F32)).astype(BF16)


def dot(a, b, over):
    return lax.dot_general(a, b, (((over,), (0,)), ((), ())), preferred_element_type=F32)


def product(a, b, over=1):
    (ah, al), (bh, bl) = a, b
    if ah.shape[over] > LANES:
        both = dot(jnp.concatenate([ah, al], 1 - over), bh, over)
        rows = ah.shape[1 - over]
        return both[:rows] + (both[rows:] + dot(ah, bl, over))
    return dot(jnp.concatenate([ah, al], over), jnp.concatenate([bh, bh], 0), over) + dot(ah, bl, over)


def reflect(x, refl, factor):
    v = split(refl)
    coeff = product(split(factor), split(product(v, split(x), over=0)))
    return x - product(v, split(coeff))


def pick(kinds, step, pieces):
    value = pieces[0]
    for at, piece in enumerate(pieces[1:], 1):
        mask = jnp.broadcast_to(kinds[step : step + 1, :], value.shape) == at
        value = jnp.where(mask, piece, value)
    return value


def shape(*dims, dtype=F32):
    return pltpu.VMEM(dims, dtype)


def near(*values, space=pltpu.VMEM):
    return [pltpu.with_memory_space_constraint(value, space) for value in values]


def vmem_call(body, outs, name, *args):
    return pl.pallas_call(
        body,
        out_shape=outs,
        in_specs=[VMEM] * len(args),
        out_specs=[VMEM] * len(outs),
        name=name,
        compiler_params=LEAN,
    )(*near(*args))


def load(vectors, reflectors, tfactors, plan, columns):
    held, lanes = reflectors.shape[0], reflectors.shape[2]
    last = tfactors.shape[1] - 1
    groups = plan.shape[0]

    def body(plan, x, v, f, kinds_ref, x_out, v_out, f_out, end_out, plan_ref, sem):
        copies = [(plan, plan_ref), (f.at[:, last], end_out), (x, x_out), (v, v_out), (f, f_out)]
        copies = [pltpu.make_async_copy(*pair, sem.at[at]) for at, pair in enumerate(copies)]
        for copy in copies:
            copy.start()
        me = lax.axis_index("col")
        kinds_ref[...] = jnp.zeros_like(kinds_ref)
        copies[0].wait()
        for step in range(groups):
            group = plan_ref[step]
            piece = (me + columns - group // held) % columns * held + group % held
            kinds_ref[step : step + 1, :] = jnp.full((1, lanes), piece, jnp.int32)
        for copy in copies[1:]:
            copy.wait()

    return pl.pallas_call(
        body,
        out_shape=[
            shape(-(-groups // 8) * 8, lanes, dtype=jnp.int32),
            shape(*vectors.shape),
            shape(*reflectors.shape),
            shape(*tfactors.shape),
            shape(held, lanes, lanes),
        ],
        in_specs=[HBM] * 4,
        out_specs=[VMEM] * 5,
        scratch_shapes=[pltpu.SMEM((groups,), jnp.int32), pltpu.SemaphoreType.DMA((5,))],
        name="load",
        compiler_params=LEAN,
    )(*near(plan, vectors, reflectors, tfactors, space=pltpu.HBM))


def is_top(odd_round):
    return (lax.axis_index("row") % 2 == 1) != odd_round


def ordered(top, low):
    first = is_top(False)
    return jnp.where(first, top, low), jnp.where(first, low, top)


def edges(x, refls, factors, kinds, step):
    height, width = x.shape
    strip = refls[0].shape[1]
    count = height // (2 * strip)
    n = len(refls)

    def body(*refs):
        kinds_ref, x_ref, refs = refs[0], refs[1], refs[2:]
        refl_refs, factor_refs = refs[:n], refs[n : 2 * n]
        coeffs, even_ref, odd_ref = refs[2 * n : 2 * n + 2], refs[2 * n + 2], refs[2 * n + 3]
        firsts, seconds, crosses, weights, projs = [], [], [], [], []
        places = [(0, 0), (count - 1, strip)]
        for at, outer in places:
            start = at * 2 * strip
            rows = slice(start, start + 2 * strip)
            side = slice(start + outer, start + outer + strip)
            firsts.append(split(pick(kinds_ref, step, [r[rows, :] for r in refl_refs])))
            seconds.append(split(pick(kinds_ref, step + 1, [r[side, :] for r in refl_refs])))
        for (at, outer), first, second in zip(places, firsts, seconds):
            crosses.append(product(second, [v[outer : outer + strip] for v in first], over=0))
        for (at, outer), first, second, coeff_ref in zip(places, firsts, seconds, coeffs):
            rows = slice(at * 2 * strip, (at + 1) * 2 * strip)
            blank = jnp.zeros((strip, strip), BF16)
            second = [jnp.concatenate([v, blank] if outer == 0 else [blank, v], 0) for v in second]
            high, low = split(x_ref[rows, :])
            all_high = dot(jnp.concatenate([*first, *second], 1), high, 0)
            all_low = dot(jnp.concatenate([first[0], second[0]], 1), low, 0)
            parts = [all_high[i * strip : (i + 1) * strip] for i in range(4)]
            coeff_ref[...] = parts[0] + (parts[1] + all_low[:strip])
            projs.append(parts[2] + (parts[3] + all_low[strip:]))
        for (at, outer), cross in zip(places, crosses):
            factor = pick(kinds_ref, step, [r[at] for r in factor_refs])
            weights.append(product(split(cross), split(factor)))
        for at, (weight, coeff_ref) in enumerate(zip(weights, coeffs)):
            projs[at] = projs[at] - product(split(weight), split(coeff_ref[...]))
        even_ref[...], odd_ref[...] = ordered(*projs)

    return vmem_call(body, [shape(strip, width)] * 4, "edges", kinds, x, *refls, *factors)


def middle(x, refls, factors, kinds, step, coeffs):
    height, width = x.shape
    strip = refls[0].shape[1]
    count = height // (2 * strip)
    n = len(refls)

    def body(*refs):
        kinds_ref, x_ref, coeff_refs, refs = refs[0], refs[1], refs[2:4], refs[4:]
        refl_refs, factor_refs = refs[:n], refs[n : 2 * n]
        out_ref, top_ref, low_ref, work_ref, sem = refs[2 * n :]
        for at in range(count):
            rows = slice(at * 2 * strip, (at + 1) * 2 * strip)
            refl = split(pick(kinds_ref, step, [r[rows, :] for r in refl_refs]))
            factor = split(pick(kinds_ref, step, [r[at] for r in factor_refs]))
            block = x_ref[rows, :]
            if at in (0, count - 1):
                coeff = coeff_refs[at // (count - 1)][...]
            else:
                coeff = product(refl, split(block), over=0)
            new = block - product(refl, split(product(factor, split(coeff))))
            work_ref[rows, :] = new
            if at == 0:
                top_ref[...] = new[:strip]
            if at == count - 1:
                low_ref[...] = new[strip:]
        copies = []
        for at in range(count - 1):
            rows = pl.ds(at * 2 * strip + strip, 2 * strip)
            refl = pick(kinds_ref, step + 1, [r[rows, :] for r in refl_refs])
            factor = pick(kinds_ref, step + 1, [r[at] for r in factor_refs])
            work_ref[rows, :] = reflect(work_ref[rows, :], refl, factor)
            copy = pltpu.make_async_copy(work_ref.at[rows, :], out_ref.at[rows, :], sem.at[at])
            copy.start()
            copies.append(copy)
        for copy in copies:
            copy.wait()

    args = near(kinds, x, *coeffs, *refls, *factors)
    return pl.pallas_call(
        body,
        out_shape=[jax.ShapeDtypeStruct((height, width), F32)] + [shape(strip, width)] * 2,
        in_specs=[VMEM] * len(args),
        out_specs=[ANY, VMEM, VMEM],
        scratch_shapes=[pltpu.VMEM((height, width), F32), pltpu.SemaphoreType.DMA((count - 1,))],
        name="middle",
        compiler_params=LEAN,
    )(*args)


def prepare(refls, factors, behind, kinds, step, strips, projs):
    height, strip = refls[0].shape
    width = strips[0].shape[1]
    count = height // (2 * strip)
    n = len(refls)

    def body(kinds_ref, top_ref, low_ref, even_ref, odd_ref, *refs):
        refl_refs, factor_refs, behind_refs = refs[:n], refs[n : 2 * n], refs[2 * n : 3 * n]
        rests, highs, lows = refs[3 * n : 3 * n + 2], refs[3 * n + 2 : 3 * n + 4], refs[3 * n + 4 :]
        row, last = lax.axis_index("row"), lax.axis_size("row") - 1
        ends = [r[count - 1] for r in factor_refs], [r[...] for r in behind_refs]
        own = ordered(even_ref[...], odd_ref[...])

        def work(start, ends, present, strip_rows, proj):
            refl = pick(kinds_ref, step + 1, [r[start : start + strip, :] for r in refl_refs])
            weight = product(split(refl), split(pick(kinds_ref, step + 1, ends)))
            weight = jnp.where(present, weight, jnp.zeros_like(weight))
            parts = split(weight)
            return strip_rows - product(parts, split(proj)), *parts

        top = work(0, ends[1], row > 0, top_ref[...], own[0])
        low = work(height - strip, ends[0], row < last, low_ref[...], own[1])
        rests[0][...], rests[1][...] = ordered(top[0], low[0])
        for at, halves in ((1, highs), (2, lows)):
            even, odd = ordered(top[at].astype(F32), low[at].astype(F32))
            halves[0][...], halves[1][...] = even.astype(BF16), odd.astype(BF16)

    rest, half = shape(strip, width), shape(strip, strip, dtype=BF16)
    outs = vmem_call(
        body,
        [rest, rest, half, half, half, half],
        "prepare",
        *(kinds, *strips, *projs, *refls, *factors, *behind),
    )
    return outs[::2], outs[1::2]


def finish(out, odd_round, rest, high, low, got):
    height, width = out.shape
    strip = rest.shape[0]

    def body(rest_ref, high_ref, low_ref, got_ref, _, out_ref, new_ref, sem):
        row, last = lax.axis_index("row"), lax.axis_size("row") - 1
        top = is_top(odd_round)
        present = jnp.where(top, row > 0, row < last)
        other = jnp.where(present, got_ref[...], jnp.zeros_like(got_ref))
        new_ref[...] = rest_ref[...] - product((high_ref[...], low_ref[...]), split(other))
        start = pl.multiple_of(jnp.where(top, 0, height - strip), strip)
        copy = pltpu.make_async_copy(new_ref, out_ref.at[pl.ds(start, strip), :], sem)
        copy.start()
        copy.wait()

    return pl.pallas_call(
        body,
        out_shape=jax.ShapeDtypeStruct((height, width), F32),
        in_specs=[VMEM] * 4 + [ANY],
        out_specs=ANY,
        scratch_shapes=[pltpu.VMEM((strip, width), F32), pltpu.SemaphoreType.DMA],
        input_output_aliases={4: 0},
        name="finish",
        compiler_params=LEAN,
    )(*near(rest, high, low, got), out)


def local(vectors, reflectors, tfactors, plan):
    groups = plan.shape[0]
    held = reflectors.shape[0]
    rows, columns = lax.axis_size("row"), lax.axis_size("col")

    def around(block, shift):
        return lax.ppermute(block, "col", [(c, (c + shift) % columns) for c in range(columns)])

    def trade(block, odd_round):
        route = []
        for row in range(rows):
            for col in range(columns):
                there = row + 1 if (row % 2 == 1) == odd_round else row - 1
                there = (there, col) if 0 <= there < rows else (row, (col + 1) % columns)
                route.append((row * columns + col, there[0] * columns + there[1]))
        return lax.ppermute(block, ("row", "col"), route)

    def others(piece):
        return [around(piece, shift) for shift in range(1, columns)]

    def apart(pieces):
        return [piece[slot] for piece in pieces for slot in range(held)]

    far_refls, far_factors = others(reflectors), others(tfactors)
    kinds, current, refl, factor, end = load(vectors, reflectors, tfactors, plan, columns)
    behind = lax.ppermute(end, "row", [(r, (r + 1) % rows) for r in range(rows)])
    refls, factors = apart([refl, *far_refls]), apart([factor, *far_factors])
    behinds = None
    for step in range(0, groups, 2):
        *coeffs, even_proj, odd_proj = edges(current, refls, factors, kinds, step)
        even_got, odd_got = trade(even_proj, False), trade(odd_proj, True)
        done, *strips = middle(current, refls, factors, kinds, step, coeffs)
        if behinds is None:
            behind, strips[0] = lax.optimization_barrier((behind, strips[0]))
            behinds = apart([behind, *others(behind)])
        even, odd = prepare(
            refls, factors, behinds, kinds, step, strips, (even_proj, odd_proj)
        )
        done = finish(done, False, *even, even_got)
        current = finish(done, True, *odd, odd_got)
    return current


def solution(mesh):
    return jax.shard_map(
        local,
        mesh=mesh,
        in_specs=(P("row", "col"), P("col", "row", None), P("col", "row", None, None), P()),
        out_specs=P("row", "col"),
        check_vma=False,
    )
```

```python
import jax
import jax.numpy as jnp
from jax import lax
from jax.experimental import pallas as pl
from jax.experimental.pallas import tpu as pltpu
from jax.sharding import PartitionSpec as P

F32 = jnp.float32
BF16 = jnp.bfloat16
LANES = 128
VMEM = pl.BlockSpec(memory_space=pltpu.VMEM)
HBM = pl.BlockSpec(memory_space=pltpu.HBM)
ANY = pl.BlockSpec(memory_space=pl.ANY)
LEAN = pltpu.CompilerParams(vmem_limit_bytes=8 << 20)


def split(a):
    high = a.astype(BF16)
    return high, (a - high.astype(F32)).astype(BF16)


def dot(a, b, over):
    return lax.dot_general(a, b, (((over,), (0,)), ((), ())), preferred_element_type=F32)


def product(a, b, over=1):
    (ah, al), (bh, bl) = a, b
    if ah.shape[over] > LANES:
        both = dot(jnp.concatenate([ah, al], 1 - over), bh, over)
        rows = ah.shape[1 - over]
        return both[:rows] + (both[rows:] + dot(ah, bl, over))
    return dot(jnp.concatenate([ah, al], over), jnp.concatenate([bh, bh], 0), over) + dot(ah, bl, over)


def pick(kinds, step, pieces):
    value = pieces[0]
    for at, piece in enumerate(pieces[1:], 1):
        mask = jnp.broadcast_to(kinds[step : step + 1, :], value.shape) == at
        value = jnp.where(mask, piece, value)
    return value


def shape(*dims, dtype=F32):
    return pltpu.VMEM(dims, dtype)


def near(*values, space=pltpu.VMEM):
    return [pltpu.with_memory_space_constraint(value, space) for value in values]


def vmem_call(body, outs, name, *args):
    return pl.pallas_call(
        body,
        out_shape=outs,
        in_specs=[VMEM] * len(args),
        out_specs=[VMEM] * len(outs),
        name=name,
        compiler_params=LEAN,
    )(*near(*args))


def load(vectors, reflectors, tfactors, plan, columns):
    held, height, lanes = reflectors.shape
    block, last = 2 * lanes, tfactors.shape[1] - 1
    groups = plan.shape[0]

    def body(plan, x, v, f, kinds_ref, x_out, v_out, f_out, end_out, plan_ref, sem):
        copies = [(plan, plan_ref), (f.at[:, last], end_out)]
        for at, place in enumerate((0, last)):
            rows = pl.ds(place * block, block)
            copies.append((v.at[:, rows], v_out.at[:, pl.ds(at * block, block)]))
            copies.append((x.at[rows], x_out.at[pl.ds(at * block, block)]))
            copies.append((f.at[:, place], f_out.at[:, at]))
        copies = [pltpu.make_async_copy(*pair, sem.at[at]) for at, pair in enumerate(copies)]
        for copy in copies:
            copy.start()
        me = lax.axis_index("col")
        kinds_ref[...] = jnp.zeros_like(kinds_ref)
        copies[0].wait()
        for step in range(groups):
            group = plan_ref[step]
            piece = (me + columns - group // held) % columns * held + group % held
            kinds_ref[step : step + 1, :] = jnp.full((1, lanes), piece, jnp.int32)
        for copy in copies[1:]:
            copy.wait()

    return pl.pallas_call(
        body,
        out_shape=[
            shape(-(-groups // 8) * 8, lanes, dtype=jnp.int32),
            shape(2 * block, vectors.shape[1]),
            shape(held, 2 * block, lanes),
            shape(held, 2, lanes, lanes),
            shape(held, lanes, lanes),
        ],
        in_specs=[HBM] * 4,
        out_specs=[VMEM] * 5,
        scratch_shapes=[pltpu.SMEM((groups,), jnp.int32), pltpu.SemaphoreType.DMA((8,))],
        name="load",
        compiler_params=LEAN,
    )(*near(plan, vectors, reflectors, tfactors, space=pltpu.HBM))


def is_top(odd_round):
    return (lax.axis_index("row") % 2 == 1) != odd_round


def ordered(top, low):
    first = is_top(False)
    return jnp.where(first, top, low), jnp.where(first, low, top)


def apart(pieces):
    return [piece.at[slot] for piece in pieces for slot in range(piece.shape[0])]


def edges(x, own, others, kinds, step):
    width = x.shape[1]
    strip = own[0].shape[2]
    count = others[0][1].shape[1]
    held = own[0].shape[0]

    def body(kinds_ref, x_ref, own_refl, own_factor, *refs):
        far_refls, far_factors = refs[: len(others)], refs[len(others) : 2 * len(others)]
        coeffs, even_ref, odd_ref = refs[-4:-2], refs[-2], refs[-1]
        firsts, seconds, crosses, weights, projs = [], [], [], [], []
        places = [(0, 0, 0), (1, count - 1, strip)]

        def refl(step, near_row, far_row, rows):
            pieces = [own_refl[slot, near_row : near_row + rows, :] for slot in range(held)]
            pieces += [r[far_row : far_row + rows, :] for r in apart(far_refls)]
            return split(pick(kinds_ref, step, pieces))

        for at, place, outer in places:
            near_row, far_row = at * 2 * strip, place * 2 * strip
            firsts.append(refl(step, near_row, far_row, 2 * strip))
            seconds.append(refl(step + 1, near_row + outer, far_row + outer, strip))
        for (_, _, outer), first, second in zip(places, firsts, seconds):
            crosses.append(product(second, [v[outer : outer + strip] for v in first], over=0))
        for (at, _, outer), first, second in zip(places, firsts, seconds):
            blank = jnp.zeros((strip, strip), BF16)
            second = [jnp.concatenate([v, blank] if outer == 0 else [blank, v], 0) for v in second]
            high, low = split(x_ref[at * 2 * strip : (at + 1) * 2 * strip, :])
            all_high = dot(jnp.concatenate([*first, *second], 1), high, 0)
            all_low = dot(jnp.concatenate([first[0], second[0]], 1), low, 0)
            parts = [all_high[i * strip : (i + 1) * strip] for i in range(4)]
            coeffs[at][...] = parts[0] + (parts[1] + all_low[:strip])
            projs.append(parts[2] + (parts[3] + all_low[strip:]))
        for (at, place, _), cross in zip(places, crosses):
            pieces = [own_factor[slot, at] for slot in range(held)]
            factor = pick(kinds_ref, step, pieces + [r[place] for r in apart(far_factors)])
            weights.append(product(split(cross), split(factor)))
        for at, weight in enumerate(weights):
            projs[at] = projs[at] - product(split(weight), split(coeffs[at][...]))
        even_ref[...], odd_ref[...] = ordered(*projs)

    far = [piece for pair in zip(*others) for piece in pair]
    return vmem_call(body, [shape(strip, width)] * 4, "edges", kinds, x, *own, *far)


def middle(x, edge_rows, own, others, kinds, step, coeffs):
    height, width = x.shape
    held, _, strip = own[0].shape
    block = 2 * strip
    count = height // block

    def body(kinds_ref, edge_ref, top_coeff, low_coeff, *refs):
        far_refls, refs = refs[: len(others)], refs[len(others) :]
        far_factors, refs = refs[: len(others)], refs[len(others) :]
        x_hbm, v_hbm, f_hbm, work_ref, top_ref, low_ref, v_own, f_own, coeff_ref, sem = refs
        inner = pl.ds(block, height - 2 * block)
        copies = [(v_hbm, v_own), (f_hbm, f_own), (x_hbm.at[inner, :], work_ref.at[inner, :])]
        copies = [pltpu.make_async_copy(*pair, sem.at[at]) for at, pair in enumerate(copies)]
        for copy in copies:
            copy.start()
        work_ref[:block, :] = edge_ref[:block, :]
        work_ref[height - block :, :] = edge_ref[block:, :]
        refls, factors = apart([v_own, *far_refls]), apart([f_own, *far_factors])
        coeff_ref[0] = top_coeff[...]
        coeff_ref[count - 1] = low_coeff[...]
        for copy in copies:
            copy.wait()

        def run(step, blocks, offset, known):
            def rows(at):
                return slice(at * block + offset, (at + 1) * block + offset)

            def refl(at):
                return split(pick(kinds_ref, step, [r[rows(at), :] for r in refls]))

            for at in blocks:
                if at not in known:
                    coeff_ref[at] = product(refl(at), split(work_ref[rows(at), :]), over=0)
            for at in blocks:
                factor = split(pick(kinds_ref, step, [r[at] for r in factors]))
                coeff_ref[at] = product(factor, split(coeff_ref[at]))
            for at in blocks:
                change = product(refl(at), split(coeff_ref[at]))
                work_ref[rows(at), :] = work_ref[rows(at), :] - change

        run(step, range(count), 0, (0, count - 1))
        top_ref[...] = work_ref[:strip, :]
        low_ref[...] = work_ref[height - strip :, :]
        run(step + 1, range(count - 1), strip, ())

    far = [piece for pair in zip(*others) for piece in pair]
    args = near(kinds, edge_rows, *coeffs, *far)
    args, specs = args + near(x, *own, space=pltpu.HBM), [VMEM] * len(args) + [HBM] * 3
    return pl.pallas_call(
        body,
        out_shape=[shape(height, width)] + [shape(strip, width)] * 2,
        in_specs=specs,
        out_specs=[VMEM] * 3,
        scratch_shapes=[
            pltpu.VMEM(own[0].shape, F32),
            pltpu.VMEM(own[1].shape, F32),
            pltpu.VMEM((count, strip, width), F32),
            pltpu.SemaphoreType.DMA((3,)),
        ],
        name="middle",
        compiler_params=LEAN,
    )(*args)


def store(work, strip):
    height, width = work.shape

    def body(work_ref, out_ref, sem):
        inner = pl.ds(strip, height - 2 * strip)
        copy = pltpu.make_async_copy(work_ref.at[inner, :], out_ref.at[inner, :], sem)
        copy.start()
        copy.wait()

    return pl.pallas_call(
        body,
        out_shape=jax.ShapeDtypeStruct((height, width), F32),
        in_specs=[VMEM],
        out_specs=ANY,
        scratch_shapes=[pltpu.SemaphoreType.DMA],
        name="store",
        compiler_params=LEAN,
    )(*near(work))


def prepare(own, others, behind, kinds, step, strips, projs):
    strip, width = strips[0].shape
    count = others[0][1].shape[1]
    height = others[0][0].shape[1]
    held = own[0].shape[0]
    far = [piece for pair in zip(*others) for piece in pair]

    def body(kinds_ref, top_ref, low_ref, even_ref, odd_ref, own_refl, own_factor, *refs):
        far_refls, refs = refs[: len(others)], refs[len(others) :]
        far_factors, refs = refs[: len(others)], refs[len(others) :]
        behinds, refs = apart(refs[: len(behind)]), refs[len(behind) :]
        rests, highs, lows = refs[:2], refs[2:4], refs[4:]
        row, last = lax.axis_index("row"), lax.axis_size("row") - 1
        projs = ordered(even_ref[...], odd_ref[...])

        def weight(near_row, far_row, ends, present):
            pieces = [own_refl[slot, near_row : near_row + strip, :] for slot in range(held)]
            pieces += [r[far_row : far_row + strip, :] for r in apart(far_refls)]
            refl = split(pick(kinds_ref, step + 1, pieces))
            value = product(refl, split(pick(kinds_ref, step + 1, ends)))
            return jnp.where(present, value, jnp.zeros_like(value))

        ends = [own_factor[slot, 1] for slot in range(held)]
        ends += [r[count - 1] for r in apart(far_factors)]
        top = weight(0, 0, [r[...] for r in behinds], row > 0)
        low = weight(3 * strip, height - strip, ends, row < last)
        even, odd = ordered(top, low)
        highs[0][...], lows[0][...] = split(even)
        highs[1][...], lows[1][...] = split(odd)
        top = top_ref[...] - product(split(top), split(projs[0]))
        low = low_ref[...] - product(split(low), split(projs[1]))
        rests[0][...], rests[1][...] = ordered(top, low)

    rest, half = shape(strip, width), shape(strip, strip, dtype=BF16)
    return vmem_call(
        body,
        [rest, rest, half, half, half, half],
        "prepare",
        *(kinds, *strips, *projs, *own, *far, *behind),
    )


def finish(out, prepared, gots):
    height, width = out.shape
    strip = gots[0].shape[0]

    def body(*refs):
        rests, highs, lows, gots = refs[:2], refs[2:4], refs[4:6], refs[6:8]
        out_ref, new_ref, sem = refs[9:]
        row, last = lax.axis_index("row"), lax.axis_size("row") - 1
        copies = []
        for at in range(2):
            top = is_top(at == 1)
            present = jnp.where(top, row > 0, row < last)
            other = jnp.where(present, gots[at][...], jnp.zeros_like(gots[at]))
            weight = highs[at][...], lows[at][...]
            new_ref[at] = rests[at][...] - product(weight, split(other))
            start = pl.multiple_of(jnp.where(top, 0, height - strip), strip)
            rows = out_ref.at[pl.ds(start, strip), :]
            copies.append(pltpu.make_async_copy(new_ref.at[at], rows, sem.at[at]))
            copies[-1].start()
        for copy in copies:
            copy.wait()

    return pl.pallas_call(
        body,
        out_shape=jax.ShapeDtypeStruct((height, width), F32),
        in_specs=[VMEM] * 8 + [ANY],
        out_specs=ANY,
        scratch_shapes=[pltpu.VMEM((2, strip, width), F32), pltpu.SemaphoreType.DMA((2,))],
        input_output_aliases={8: 0},
        name="finish",
        compiler_params=LEAN,
    )(*near(*prepared, *gots), out)


def local(vectors, reflectors, tfactors, plan):
    groups, strip = plan.shape[0], reflectors.shape[2]
    rows, columns = lax.axis_size("row"), lax.axis_size("col")

    def around(block, shift):
        return lax.ppermute(block, "col", [(c, (c + shift) % columns) for c in range(columns)])

    def trade(block, odd_round):
        route = []
        for row in range(rows):
            for col in range(columns):
                there = row + 1 if (row % 2 == 1) == odd_round else row - 1
                there = (there, col) if 0 <= there < rows else (row, (col + 1) % columns)
                route.append((row * columns + col, there[0] * columns + there[1]))
        return lax.ppermute(block, ("row", "col"), route)

    shifts = range(1, columns)
    others = [(around(reflectors, shift), around(tfactors, shift)) for shift in shifts]
    current, behinds = vectors, None
    for step in range(0, groups, 2):
        kinds, edge_rows, *own, end = load(current, reflectors, tfactors, plan, columns)
        if behinds is None:
            behind = lax.ppermute(end, "row", [(r, (r + 1) % rows) for r in range(rows)])
        *coeffs, even_proj, odd_proj = edges(edge_rows, own, others, kinds, step)
        gots = trade(even_proj, False), trade(odd_proj, True)
        work, *strips = middle(
            current, edge_rows, (reflectors, tfactors), others, kinds, step, coeffs
        )
        if behinds is None:
            behind, strips[0] = lax.optimization_barrier((behind, strips[0]))
            behinds = [behind, *(around(behind, shift) for shift in shifts)]
        out = store(work, strip)
        prepared = prepare(own, others, behinds, kinds, step, strips, (even_proj, odd_proj))
        current = finish(out, prepared, gots)
    return current


def solution(mesh):
    return jax.shard_map(
        local,
        mesh=mesh,
        in_specs=(P("row", "col"), P("col", "row", None), P("col", "row", None, None), P()),
        out_specs=P("row", "col"),
        check_vma=False,
    )
```

```python
import jax
import jax.numpy as jnp
from jax import lax
from jax.experimental import pallas as pl
from jax.experimental.pallas import tpu as pltpu
from jax.sharding import PartitionSpec as P

F32 = jnp.float32
BF16 = jnp.bfloat16
LANES = 128
VMEM = pl.BlockSpec(memory_space=pltpu.VMEM)
HBM = pl.BlockSpec(memory_space=pltpu.HBM)
ANY = pl.BlockSpec(memory_space=pl.ANY)
LEAN = pltpu.CompilerParams(vmem_limit_bytes=8 << 20)


def split(a):
    high = a.astype(BF16)
    return high, (a - high.astype(F32)).astype(BF16)


def dot(a, b, over):
    return lax.dot_general(a, b, (((over,), (0,)), ((), ())), preferred_element_type=F32)


def product(a, b, over=1):
    (ah, al), (bh, bl) = a, b
    if ah.shape[over] > LANES:
        both = dot(jnp.concatenate([ah, al], 1 - over), bh, over)
        rows = ah.shape[1 - over]
        return both[:rows] + (both[rows:] + dot(ah, bl, over))
    return dot(jnp.concatenate([ah, al], over), jnp.concatenate([bh, bh], 0), over) + dot(ah, bl, over)


def pick(kinds, step, pieces):
    value = pieces[0]
    for at, piece in enumerate(pieces[1:], 1):
        mask = jnp.broadcast_to(kinds[step : step + 1, :], value.shape) == at
        value = jnp.where(mask, piece, value)
    return value


def shape(*dims, dtype=F32):
    return pltpu.VMEM(dims, dtype)


def near(*values, space=pltpu.VMEM):
    return [pltpu.with_memory_space_constraint(value, space) for value in values]


def vmem_call(body, outs, name, *args):
    return pl.pallas_call(
        body,
        out_shape=outs,
        in_specs=[VMEM] * len(args),
        out_specs=[VMEM] * len(outs),
        name=name,
        compiler_params=LEAN,
    )(*near(*args))


def load(vectors, reflectors, tfactors, plan, columns):
    held, height, lanes = reflectors.shape
    block, last = 2 * lanes, tfactors.shape[1] - 1
    groups = plan.shape[0]

    def body(plan, x, v, f, kinds_ref, x_out, v_out, f_out, end_out, plan_ref, sem):
        copies = [(plan, plan_ref), (f.at[:, last], end_out)]
        for at, place in enumerate((0, last)):
            rows = pl.ds(place * block, block)
            copies.append((v.at[:, rows], v_out.at[:, pl.ds(at * block, block)]))
            copies.append((x.at[rows], x_out.at[pl.ds(at * block, block)]))
            copies.append((f.at[:, place], f_out.at[:, at]))
        copies = [pltpu.make_async_copy(*pair, sem.at[at]) for at, pair in enumerate(copies)]
        for copy in copies:
            copy.start()
        me = lax.axis_index("col")
        kinds_ref[...] = jnp.zeros_like(kinds_ref)
        copies[0].wait()
        for step in range(groups):
            group = plan_ref[step]
            piece = (me + columns - group // held) % columns * held + group % held
            kinds_ref[step : step + 1, :] = jnp.full((1, lanes), piece, jnp.int32)
        for copy in copies[1:]:
            copy.wait()

    return pl.pallas_call(
        body,
        out_shape=[
            shape(-(-groups // 8) * 8, lanes, dtype=jnp.int32),
            shape(2 * block, vectors.shape[1]),
            shape(held, 2 * block, lanes),
            shape(held, 2, lanes, lanes),
            shape(held, lanes, lanes),
        ],
        in_specs=[HBM] * 4,
        out_specs=[VMEM] * 5,
        scratch_shapes=[pltpu.SMEM((groups,), jnp.int32), pltpu.SemaphoreType.DMA((8,))],
        name="load",
        compiler_params=LEAN,
    )(*near(plan, vectors, reflectors, tfactors, space=pltpu.HBM))


def is_top(odd_round):
    return (lax.axis_index("row") % 2 == 1) != odd_round


def ordered(top, low):
    first = is_top(False)
    return jnp.where(first, top, low), jnp.where(first, low, top)


def apart(pieces):
    return [piece.at[slot] for piece in pieces for slot in range(piece.shape[0])]


def edge(x, own, others, kinds, step, odd_round):
    width = x.shape[1]
    held, _, strip = own[0].shape
    block = 2 * strip
    height, count = others[0][0].shape[1], others[0][1].shape[1]

    def body(kinds_ref, x_ref, own_refl, own_factor, *refs):
        far_refls, far_factors = refs[: len(others)], refs[len(others) : -2]
        coeff_ref, proj_ref = refs[-2:]
        top = is_top(odd_round)
        near_rows = pl.ds(pl.multiple_of(jnp.where(top, 0, block), block), block)
        far_rows = pl.ds(pl.multiple_of(jnp.where(top, 0, height - block), block), block)
        slots = range(held)

        def refl(step):
            pieces = [own_refl[slot, near_rows, :] for slot in slots]
            return pick(kinds_ref, step, pieces + [r[far_rows, :] for r in apart(far_refls)])

        row = lax.broadcasted_iota(jnp.int32, (block, strip), 0) - jnp.where(top, 0, strip)
        second = jnp.where((row >= 0) & (row < strip), refl(step + 1), 0.0)
        first, second = split(refl(step)), split(second)
        high, low = split(x_ref[near_rows, :])
        cross = product(second, first, over=0)
        all_high = dot(jnp.concatenate([*first, *second], 1), high, 0)
        all_low = dot(jnp.concatenate([first[0], second[0]], 1), low, 0)
        pieces = [own_factor[slot, jnp.where(top, 0, 1)] for slot in slots]
        pieces += [r[jnp.where(top, 0, count - 1)] for r in apart(far_factors)]
        weight = product(split(cross), split(pick(kinds_ref, step, pieces)))
        parts = [all_high[i * strip : (i + 1) * strip] for i in range(4)]
        coeff = parts[0] + (parts[1] + all_low[:strip])
        coeff_ref[...] = coeff
        rest = product(split(weight), split(coeff))
        proj_ref[...] = parts[2] + (parts[3] + all_low[strip:]) - rest

    far = [piece for pair in zip(*others) for piece in pair]
    return vmem_call(body, [shape(strip, width)] * 2, "edge", kinds, x, *own, *far)


def middle(x, edge_rows, own, others, kinds, step, coeffs):
    height, width = x.shape
    held, _, strip = own[0].shape
    block = 2 * strip
    count = height // block

    def body(kinds_ref, edge_ref, even_coeff, odd_coeff, *refs):
        far_refls, refs = refs[: len(others)], refs[len(others) :]
        far_factors, refs = refs[: len(others)], refs[len(others) :]
        x_hbm, v_hbm, f_hbm, work_ref, top_ref, low_ref, v_own, f_own, coeff_ref, sem = refs
        inner = pl.ds(block, height - 2 * block)
        copies = [(v_hbm, v_own), (f_hbm, f_own), (x_hbm.at[inner, :], work_ref.at[inner, :])]
        copies = [pltpu.make_async_copy(*pair, sem.at[at]) for at, pair in enumerate(copies)]
        for copy in copies:
            copy.start()
        work_ref[:block, :] = edge_ref[:block, :]
        work_ref[height - block :, :] = edge_ref[block:, :]
        refls, factors = apart([v_own, *far_refls]), apart([f_own, *far_factors])
        coeff_ref[0], coeff_ref[count - 1] = ordered(even_coeff[...], odd_coeff[...])
        for copy in copies:
            copy.wait()

        def run(step, blocks, offset, known):
            def rows(at):
                return slice(at * block + offset, (at + 1) * block + offset)

            def refl(at):
                return split(pick(kinds_ref, step, [r[rows(at), :] for r in refls]))

            for at in blocks:
                if at not in known:
                    coeff_ref[at] = product(refl(at), split(work_ref[rows(at), :]), over=0)
            for at in blocks:
                factor = split(pick(kinds_ref, step, [r[at] for r in factors]))
                coeff_ref[at] = product(factor, split(coeff_ref[at]))
            for at in blocks:
                change = product(refl(at), split(coeff_ref[at]))
                work_ref[rows(at), :] = work_ref[rows(at), :] - change

        run(step, range(count), 0, (0, count - 1))
        top_ref[...] = work_ref[:strip, :]
        low_ref[...] = work_ref[height - strip :, :]
        run(step + 1, range(count - 1), strip, ())

    far = [piece for pair in zip(*others) for piece in pair]
    args = near(kinds, edge_rows, *coeffs, *far)
    args, specs = args + near(x, *own, space=pltpu.HBM), [VMEM] * len(args) + [HBM] * 3
    return pl.pallas_call(
        body,
        out_shape=[shape(height, width)] + [shape(strip, width)] * 2,
        in_specs=specs,
        out_specs=[VMEM] * 3,
        scratch_shapes=[
            pltpu.VMEM(own[0].shape, F32),
            pltpu.VMEM(own[1].shape, F32),
            pltpu.VMEM((count, strip, width), F32),
            pltpu.SemaphoreType.DMA((3,)),
        ],
        name="middle",
        compiler_params=LEAN,
    )(*args)


def store(work, strip):
    height, width = work.shape

    def body(work_ref, out_ref, sem):
        inner = pl.ds(strip, height - 2 * strip)
        copy = pltpu.make_async_copy(work_ref.at[inner, :], out_ref.at[inner, :], sem)
        copy.start()
        copy.wait()

    return pl.pallas_call(
        body,
        out_shape=jax.ShapeDtypeStruct((height, width), F32),
        in_specs=[VMEM],
        out_specs=ANY,
        scratch_shapes=[pltpu.SemaphoreType.DMA],
        name="store",
        compiler_params=LEAN,
    )(*near(work))


def prepare(own, others, behind, kinds, step, strips, projs):
    strip, width = strips[0].shape
    count = others[0][1].shape[1]
    height = others[0][0].shape[1]
    held = own[0].shape[0]
    far = [piece for pair in zip(*others) for piece in pair]

    def body(kinds_ref, top_ref, low_ref, even_ref, odd_ref, own_refl, own_factor, *refs):
        far_refls, refs = refs[: len(others)], refs[len(others) :]
        far_factors, refs = refs[: len(others)], refs[len(others) :]
        behinds, refs = apart(refs[: len(behind)]), refs[len(behind) :]
        rests, highs, lows = refs[:2], refs[2:4], refs[4:]
        row, last = lax.axis_index("row"), lax.axis_size("row") - 1
        projs = ordered(even_ref[...], odd_ref[...])

        def weight(near_row, far_row, ends, present):
            pieces = [own_refl[slot, near_row : near_row + strip, :] for slot in range(held)]
            pieces += [r[far_row : far_row + strip, :] for r in apart(far_refls)]
            refl = split(pick(kinds_ref, step + 1, pieces))
            value = product(refl, split(pick(kinds_ref, step + 1, ends)))
            return jnp.where(present, value, jnp.zeros_like(value))

        ends = [own_factor[slot, 1] for slot in range(held)]
        ends += [r[count - 1] for r in apart(far_factors)]
        top = weight(0, 0, [r[...] for r in behinds], row > 0)
        low = weight(3 * strip, height - strip, ends, row < last)
        even, odd = ordered(top, low)
        highs[0][...], lows[0][...] = split(even)
        highs[1][...], lows[1][...] = split(odd)
        top = top_ref[...] - product(split(top), split(projs[0]))
        low = low_ref[...] - product(split(low), split(projs[1]))
        rests[0][...], rests[1][...] = ordered(top, low)

    rest, half = shape(strip, width), shape(strip, strip, dtype=BF16)
    return vmem_call(
        body,
        [rest, rest, half, half, half, half],
        "prepare",
        *(kinds, *strips, *projs, *own, *far, *behind),
    )


def finish(out, prepared, gots):
    height, width = out.shape
    strip = gots[0].shape[0]

    def body(*refs):
        rests, highs, lows, gots = refs[:2], refs[2:4], refs[4:6], refs[6:8]
        out_ref, new_ref, sem = refs[9:]
        row, last = lax.axis_index("row"), lax.axis_size("row") - 1
        copies = []
        for at in range(2):
            top = is_top(at == 1)
            present = jnp.where(top, row > 0, row < last)
            other = jnp.where(present, gots[at][...], jnp.zeros_like(gots[at]))
            weight = highs[at][...], lows[at][...]
            new_ref[at] = rests[at][...] - product(weight, split(other))
            start = pl.multiple_of(jnp.where(top, 0, height - strip), strip)
            rows = out_ref.at[pl.ds(start, strip), :]
            copies.append(pltpu.make_async_copy(new_ref.at[at], rows, sem.at[at]))
            copies[-1].start()
        for copy in copies:
            copy.wait()

    return pl.pallas_call(
        body,
        out_shape=jax.ShapeDtypeStruct((height, width), F32),
        in_specs=[VMEM] * 8 + [ANY],
        out_specs=ANY,
        scratch_shapes=[pltpu.VMEM((2, strip, width), F32), pltpu.SemaphoreType.DMA((2,))],
        input_output_aliases={8: 0},
        name="finish",
        compiler_params=LEAN,
    )(*near(*prepared, *gots), out)


def local(vectors, reflectors, tfactors, plan):
    groups, strip = plan.shape[0], reflectors.shape[2]
    rows, columns = lax.axis_size("row"), lax.axis_size("col")

    def around(block, shift):
        return lax.ppermute(block, "col", [(c, (c + shift) % columns) for c in range(columns)])

    def trade(block, odd_round):
        route = []
        for row in range(rows):
            for col in range(columns):
                there = row + 1 if (row % 2 == 1) == odd_round else row - 1
                there = (there, col) if 0 <= there < rows else (row, (col + 1) % columns)
                route.append((row * columns + col, there[0] * columns + there[1]))
        return lax.ppermute(block, ("row", "col"), route)

    shifts = range(1, columns)
    others = [(around(reflectors, shift), around(tfactors, shift)) for shift in shifts]
    current, behinds = vectors, None
    for step in range(0, groups, 2):
        kinds, edge_rows, *own, end = load(current, reflectors, tfactors, plan, columns)
        if behinds is None:
            behind = lax.ppermute(end, "row", [(r, (r + 1) % rows) for r in range(rows)])
        coeffs, projs, gots = [], [], []
        for odd_round in (False, True):
            coeff, proj = edge(edge_rows, own, others, kinds, step, odd_round)
            coeffs.append(coeff)
            projs.append(proj)
            gots.append(trade(proj, odd_round))
        work, *strips = middle(
            current, edge_rows, (reflectors, tfactors), others, kinds, step, coeffs
        )
        if behinds is None:
            behind, strips[0] = lax.optimization_barrier((behind, strips[0]))
            behinds = [behind, *(around(behind, shift) for shift in shifts)]
        out = store(work, strip)
        prepared = prepare(own, others, behinds, kinds, step, strips, projs)
        current = finish(out, prepared, gots)
    return current


def solution(mesh):
    return jax.shard_map(
        local,
        mesh=mesh,
        in_specs=(P("row", "col"), P("col", "row", None), P("col", "row", None, None), P()),
        out_specs=P("row", "col"),
        check_vma=False,
    )
```

```python
import jax
import jax.numpy as jnp
from jax import lax
from jax.experimental import pallas as pl
from jax.experimental.pallas import tpu as pltpu
from jax.sharding import PartitionSpec as P

F32 = jnp.float32
BF16 = jnp.bfloat16
LANES = 128
VMEM = pl.BlockSpec(memory_space=pltpu.VMEM)
HBM = pl.BlockSpec(memory_space=pltpu.HBM)
ANY = pl.BlockSpec(memory_space=pl.ANY)
LEAN = pltpu.CompilerParams(vmem_limit_bytes=8 << 20)


def split(a):
    high = a.astype(BF16)
    return high, (a - high.astype(F32)).astype(BF16)


def dot(a, b, over):
    return lax.dot_general(a, b, (((over,), (0,)), ((), ())), preferred_element_type=F32)


def product(a, b, over=1):
    (ah, al), (bh, bl) = a, b
    if ah.shape[over] > LANES:
        both = dot(jnp.concatenate([ah, al], 1 - over), bh, over)
        rows = ah.shape[1 - over]
        return both[:rows] + (both[rows:] + dot(ah, bl, over))
    return dot(jnp.concatenate([ah, al], over), jnp.concatenate([bh, bh], 0), over) + dot(ah, bl, over)


def pick(kinds, step, pieces):
    value = pieces[0]
    for at, piece in enumerate(pieces[1:], 1):
        mask = jnp.broadcast_to(kinds[step : step + 1, :], value.shape) == at
        value = jnp.where(mask, piece, value)
    return value


def shape(*dims, dtype=F32):
    return pltpu.VMEM(dims, dtype)


def near(*values, space=pltpu.VMEM):
    return [pltpu.with_memory_space_constraint(value, space) for value in values]


def vmem_call(body, outs, name, *args):
    return pl.pallas_call(
        body,
        out_shape=outs,
        in_specs=[VMEM] * len(args),
        out_specs=[VMEM] * len(outs),
        name=name,
        compiler_params=LEAN,
    )(*near(*args))


def load(vectors, reflectors, tfactors, plan, columns):
    held, count, lanes = tfactors.shape[:3]
    groups = plan.shape[0]

    def body(plan, x, v, f, kinds_ref, f_out, end_out, plan_ref, sem):
        copies = [(plan, plan_ref), (f.at[:, count - 1], end_out), (f, f_out)]
        copies = [pltpu.make_async_copy(*pair, sem.at[at]) for at, pair in enumerate(copies)]
        for copy in copies:
            copy.start()
        me = lax.axis_index("col")
        kinds_ref[...] = jnp.zeros_like(kinds_ref)
        copies[0].wait()
        for step in range(groups):
            group = plan_ref[step]
            piece = (me + columns - group // held) % columns * held + group % held
            kinds_ref[step : step + 1, :] = jnp.full((1, lanes), piece, jnp.int32)
        for copy in copies[1:]:
            copy.wait()

    return pl.pallas_call(
        body,
        out_shape=[
            shape(-(-groups // 8) * 8, lanes, dtype=jnp.int32),
            shape(*tfactors.shape),
            shape(held, lanes, lanes),
        ],
        in_specs=[HBM] * 4,
        out_specs=[VMEM] * 3,
        scratch_shapes=[pltpu.SMEM((groups,), jnp.int32), pltpu.SemaphoreType.DMA((3,))],
        name="load",
        compiler_params=LEAN,
    )(*near(plan, vectors, reflectors, tfactors, space=pltpu.HBM))


def is_top(odd_round):
    return (lax.axis_index("row") % 2 == 1) != odd_round


def ordered(top, low):
    first = is_top(False)
    return jnp.where(first, top, low), jnp.where(first, low, top)


def apart(pieces):
    return [piece.at[slot] for piece in pieces for slot in range(piece.shape[0])]


def edge(x, refls, factors, kinds, step, odd_round):
    width, strip = x.shape[1], refls[0].shape[2]
    block = 2 * strip
    count = factors[0].shape[1]
    n = len(refls)

    def body(kinds_ref, x_ref, *refs):
        refl_refs, factor_refs = apart(refs[:n]), apart(refs[n : 2 * n])
        coeff_ref, proj_ref = refs[-2:]

        def work(at, outer):
            start = at * block
            rows, side = slice(start, start + block), slice(start + outer, start + outer + strip)
            first = split(pick(kinds_ref, step, [r[rows, :] for r in refl_refs]))
            second = split(pick(kinds_ref, step + 1, [r[side, :] for r in refl_refs]))
            high, low = split(x_ref[rows, :])
            cross = product(second, [v[outer : outer + strip] for v in first], over=0)
            blank = jnp.zeros((strip, strip), BF16)
            second = [jnp.concatenate([v, blank] if outer == 0 else [blank, v], 0) for v in second]
            all_high = dot(jnp.concatenate([*first, *second], 1), high, 0)
            all_low = dot(jnp.concatenate([first[0], second[0]], 1), low, 0)
            factor = pick(kinds_ref, step, [r[at] for r in factor_refs])
            weight = product(split(cross), split(factor))
            parts = [all_high[i * strip : (i + 1) * strip] for i in range(4)]
            coeff = parts[0] + (parts[1] + all_low[:strip])
            coeff_ref[...] = coeff
            rest = product(split(weight), split(coeff))
            proj_ref[...] = parts[2] + (parts[3] + all_low[strip:]) - rest

        top = is_top(odd_round)
        pl.when(top)(lambda: work(0, 0))
        pl.when(jnp.logical_not(top))(lambda: work(count - 1, strip))

    args = (kinds, x, *refls, *factors)
    return vmem_call(body, [shape(strip, width)] * 2, "edge", *args)


def middle(x, refls, factors, kinds, step, coeffs):
    height, width = x.shape
    strip = refls[0].shape[2]
    block = 2 * strip
    count = height // block
    n = len(refls)

    def body(kinds_ref, x_ref, even_coeff, odd_coeff, *refs):
        refl_refs, factor_refs = apart(refs[:n]), apart(refs[n : 2 * n])
        work_ref, top_ref, low_ref, coeff_ref = refs[2 * n :]
        coeff_ref[0], coeff_ref[count - 1] = ordered(even_coeff[...], odd_coeff[...])

        def run(step, source, blocks, offset, known):
            def rows(at):
                return slice(at * block + offset, (at + 1) * block + offset)

            def refl(at):
                return split(pick(kinds_ref, step, [r[rows(at), :] for r in refl_refs]))

            for at in blocks:
                if at not in known:
                    coeff_ref[at] = product(refl(at), split(source[rows(at), :]), over=0)
            for at in blocks:
                factor = split(pick(kinds_ref, step, [r[at] for r in factor_refs]))
                coeff_ref[at] = product(factor, split(coeff_ref[at]))
            for at in blocks:
                change = product(refl(at), split(coeff_ref[at]))
                work_ref[rows(at), :] = source[rows(at), :] - change

        run(step, x_ref, range(count), 0, (0, count - 1))
        top_ref[...] = work_ref[:strip, :]
        low_ref[...] = work_ref[height - strip :, :]
        run(step + 1, work_ref, range(count - 1), strip, ())

    args = near(kinds, x, *coeffs, *refls, *factors)
    return pl.pallas_call(
        body,
        out_shape=[shape(height, width)] + [shape(strip, width)] * 2,
        in_specs=[VMEM] * len(args),
        out_specs=[VMEM] * 3,
        scratch_shapes=[pltpu.VMEM((count, strip, width), F32)],
        name="middle",
        compiler_params=LEAN,
    )(*args)


def store(work, strip):
    height, width = work.shape

    def body(work_ref, out_ref, sem):
        inner = pl.ds(strip, height - 2 * strip)
        copy = pltpu.make_async_copy(work_ref.at[inner, :], out_ref.at[inner, :], sem)
        copy.start()
        copy.wait()

    return pl.pallas_call(
        body,
        out_shape=jax.ShapeDtypeStruct((height, width), F32),
        in_specs=[VMEM],
        out_specs=ANY,
        scratch_shapes=[pltpu.SemaphoreType.DMA],
        name="store",
        compiler_params=LEAN,
    )(*near(work))


def prepare(refls, factors, behind, kinds, step, strips, projs):
    strip, width = strips[0].shape
    height, count = refls[0].shape[1], factors[0].shape[1]
    n = len(refls)

    def body(kinds_ref, top_ref, low_ref, even_ref, odd_ref, *refs):
        refl_refs, factor_refs = apart(refs[:n]), apart(refs[n : 2 * n])
        behind_refs, refs = apart(refs[2 * n : 3 * n]), refs[3 * n :]
        rests, highs, lows = refs[:2], refs[2:4], refs[4:]
        row, last = lax.axis_index("row"), lax.axis_size("row") - 1
        projs = ordered(even_ref[...], odd_ref[...])

        def weight(start, ends, present):
            refl = pick(kinds_ref, step + 1, [r[start : start + strip, :] for r in refl_refs])
            value = product(split(refl), split(pick(kinds_ref, step + 1, ends)))
            return jnp.where(present, value, jnp.zeros_like(value))

        top = weight(0, [r[...] for r in behind_refs], row > 0)
        low = weight(height - strip, [r[count - 1] for r in factor_refs], row < last)
        even, odd = ordered(top, low)
        highs[0][...], lows[0][...] = split(even)
        highs[1][...], lows[1][...] = split(odd)
        top = top_ref[...] - product(split(top), split(projs[0]))
        low = low_ref[...] - product(split(low), split(projs[1]))
        rests[0][...], rests[1][...] = ordered(top, low)

    rest, half = shape(strip, width), shape(strip, strip, dtype=BF16)
    return vmem_call(
        body,
        [rest, rest, half, half, half, half],
        "prepare",
        *(kinds, *strips, *projs, *refls, *factors, *behind),
    )


def finish(out, prepared, gots):
    height, width = out.shape
    strip = gots[0].shape[0]

    def body(*refs):
        rests, highs, lows, gots = refs[:2], refs[2:4], refs[4:6], refs[6:8]
        out_ref, new_ref, sem = refs[9:]
        row, last = lax.axis_index("row"), lax.axis_size("row") - 1
        copies = []
        for at in range(2):
            top = is_top(at == 1)
            present = jnp.where(top, row > 0, row < last)
            other = jnp.where(present, gots[at][...], jnp.zeros_like(gots[at]))
            weight = highs[at][...], lows[at][...]
            new_ref[at] = rests[at][...] - product(weight, split(other))
            start = pl.multiple_of(jnp.where(top, 0, height - strip), strip)
            rows = out_ref.at[pl.ds(start, strip), :]
            copies.append(pltpu.make_async_copy(new_ref.at[at], rows, sem.at[at]))
            copies[-1].start()
        for copy in copies:
            copy.wait()

    return pl.pallas_call(
        body,
        out_shape=jax.ShapeDtypeStruct((height, width), F32),
        in_specs=[VMEM] * 8 + [ANY],
        out_specs=ANY,
        scratch_shapes=[pltpu.VMEM((2, strip, width), F32), pltpu.SemaphoreType.DMA((2,))],
        input_output_aliases={8: 0},
        name="finish",
        compiler_params=LEAN,
    )(*near(*prepared, *gots), out)


def local(vectors, reflectors, tfactors, plan):
    groups, strip = plan.shape[0], reflectors.shape[2]
    rows, columns = lax.axis_size("row"), lax.axis_size("col")

    def around(block, shift):
        return lax.ppermute(block, "col", [(c, (c + shift) % columns) for c in range(columns)])

    def trade(block, odd_round):
        route = []
        for row in range(rows):
            for col in range(columns):
                there = row + 1 if (row % 2 == 1) == odd_round else row - 1
                there = (there, col) if 0 <= there < rows else (row, (col + 1) % columns)
                route.append((row * columns + col, there[0] * columns + there[1]))
        return lax.ppermute(block, ("row", "col"), route)

    def everyone(mine, sent):
        return [mine, *(around(sent, shift) for shift in range(1, columns))]

    kinds, factor, end = load(vectors, reflectors, tfactors, plan, columns)
    refls, factors = everyone(reflectors, reflectors), everyone(factor, tfactors)
    behind = lax.ppermute(end, "row", [(r, (r + 1) % rows) for r in range(rows)])
    current, behinds = vectors, None
    for step in range(0, groups, 2):
        coeffs, projs, gots = [], [], []
        for odd_round in (False, True):
            coeff, proj = edge(current, refls, factors, kinds, step, odd_round)
            coeffs.append(coeff)
            projs.append(proj)
            gots.append(trade(proj, odd_round))
        work, *strips = middle(current, refls, factors, kinds, step, coeffs)
        if behinds is None:
            behind, strips[0] = lax.optimization_barrier((behind, strips[0]))
            behinds = everyone(behind, behind)
        out = store(work, strip)
        prepared = prepare(refls, factors, behinds, kinds, step, strips, projs)
        current = finish(out, prepared, gots)
    return current


def solution(mesh):
    return jax.shard_map(
        local,
        mesh=mesh,
        in_specs=(P("row", "col"), P("col", "row", None), P("col", "row", None, None), P()),
        out_specs=P("row", "col"),
        check_vma=False,
    )
```

```python
import jax
import jax.numpy as jnp
from jax import lax
from jax.experimental import pallas as pl
from jax.experimental.pallas import tpu as pltpu
from jax.sharding import PartitionSpec as P

F32 = jnp.float32
BF16 = jnp.bfloat16
LANES = 128
VMEM = pl.BlockSpec(memory_space=pltpu.VMEM)
HBM = pl.BlockSpec(memory_space=pltpu.HBM)
ANY = pl.BlockSpec(memory_space=pl.ANY)
LEAN = pltpu.CompilerParams(vmem_limit_bytes=8 << 20)


def split(a):
    high = a.astype(BF16)
    return high, (a - high.astype(F32)).astype(BF16)


def dot(a, b, over):
    return lax.dot_general(a, b, (((over,), (0,)), ((), ())), preferred_element_type=F32)


def product(a, b, over=1):
    (ah, al), (bh, bl) = a, b
    if ah.shape[over] > LANES:
        both = dot(jnp.concatenate([ah, al], 1 - over), bh, over)
        rows = ah.shape[1 - over]
        return both[:rows] + (both[rows:] + dot(ah, bl, over))
    return dot(jnp.concatenate([ah, al], over), jnp.concatenate([bh, bh], 0), over) + dot(ah, bl, over)


def pick(kinds, step, pieces):
    value = pieces[0]
    for at, piece in enumerate(pieces[1:], 1):
        mask = jnp.broadcast_to(kinds[step : step + 1, :], value.shape) == at
        value = jnp.where(mask, piece, value)
    return value


def shape(*dims, dtype=F32):
    return pltpu.VMEM(dims, dtype)


def near(*values, space=pltpu.VMEM):
    return [pltpu.with_memory_space_constraint(value, space) for value in values]


def vmem_call(body, outs, name, *args):
    return pl.pallas_call(
        body,
        out_shape=outs,
        in_specs=[VMEM] * len(args),
        out_specs=[VMEM] * len(outs),
        name=name,
        compiler_params=LEAN,
    )(*near(*args))


def entry(*arrays):
    lanes = (8, LANES)

    def body(*refs):
        refs[-1][...] = jnp.zeros(lanes, F32)

    return pl.pallas_call(
        body,
        out_shape=shape(*lanes),
        in_specs=[HBM] * len(arrays),
        out_specs=VMEM,
        name="entry",
        compiler_params=LEAN,
    )(*near(*arrays, space=pltpu.HBM))


def tables(mark, tfactors, plan, columns):
    held, count, lanes = tfactors.shape[:3]
    groups = plan.shape[1]

    def body(_, plan_ref, f_ref, kinds_ref, end_ref):
        end_ref[...] = f_ref[:, count - 1]
        me = lax.axis_index("col")
        kinds_ref[...] = jnp.zeros_like(kinds_ref)
        for step in range(groups):
            group = jnp.broadcast_to(plan_ref[:, step : step + 1], (1, lanes))
            home = group // held if held > 1 else group
            gap = me - home
            gap = jnp.where(gap < 0, gap + columns, gap)
            kinds_ref[step : step + 1, :] = gap * held + (group - home * held)

    table = shape(-(-groups // 8) * 8, lanes, dtype=jnp.int32)
    return vmem_call(body, [table, shape(held, lanes, lanes)], "tables", mark, plan, tfactors)


def is_top(odd_round):
    return (lax.axis_index("row") % 2 == 1) != odd_round


def ordered(top, low):
    first = is_top(False)
    return jnp.where(first, top, low), jnp.where(first, low, top)


def apart(pieces):
    return [piece.at[slot] for piece in pieces for slot in range(piece.shape[0])]


def edge(x, refls, factors, kinds, step, odd_round):
    width, strip = x.shape[1], refls[0].shape[2]
    block = 2 * strip
    count = factors[0].shape[1]
    n = len(refls)

    def body(kinds_ref, x_ref, *refs):
        refl_refs, factor_refs = apart(refs[:n]), apart(refs[n : 2 * n])
        coeff_ref, proj_ref = refs[-2:]

        def work(at, outer):
            start = at * block
            rows, side = slice(start, start + block), slice(start + outer, start + outer + strip)
            first = split(pick(kinds_ref, step, [r[rows, :] for r in refl_refs]))
            second = split(pick(kinds_ref, step + 1, [r[side, :] for r in refl_refs]))
            high, low = split(x_ref[rows, :])
            cross = product(second, [v[outer : outer + strip] for v in first], over=0)
            blank = jnp.zeros((strip, strip), BF16)
            second = [jnp.concatenate([v, blank] if outer == 0 else [blank, v], 0) for v in second]
            all_high = dot(jnp.concatenate([*first, *second], 1), high, 0)
            all_low = dot(jnp.concatenate([first[0], second[0]], 1), low, 0)
            factor = pick(kinds_ref, step, [r[at] for r in factor_refs])
            weight = product(split(cross), split(factor))
            parts = [all_high[i * strip : (i + 1) * strip] for i in range(4)]
            coeff = parts[0] + (parts[1] + all_low[:strip])
            coeff_ref[...] = coeff
            rest = product(split(weight), split(coeff))
            proj_ref[...] = parts[2] + (parts[3] + all_low[strip:]) - rest

        top = is_top(odd_round)
        pl.when(top)(lambda: work(0, 0))
        pl.when(jnp.logical_not(top))(lambda: work(count - 1, strip))

    args = (kinds, x, *refls, *factors)
    return vmem_call(body, [shape(strip, width)] * 2, "edge", *args)


def middle(x, refls, factors, kinds, step, coeffs):
    height, width = x.shape
    strip = refls[0].shape[2]
    block = 2 * strip
    count = height // block
    n = len(refls)

    def body(kinds_ref, x_ref, even_coeff, odd_coeff, *refs):
        refl_refs, factor_refs = apart(refs[:n]), apart(refs[n : 2 * n])
        work_ref, top_ref, low_ref, coeff_ref = refs[2 * n :]
        coeff_ref[0], coeff_ref[count - 1] = ordered(even_coeff[...], odd_coeff[...])

        def run(step, source, blocks, offset, known):
            def rows(at):
                return slice(at * block + offset, (at + 1) * block + offset)

            def refl(at):
                return split(pick(kinds_ref, step, [r[rows(at), :] for r in refl_refs]))

            for at in blocks:
                if at not in known:
                    coeff_ref[at] = product(refl(at), split(source[rows(at), :]), over=0)
            for at in blocks:
                factor = split(pick(kinds_ref, step, [r[at] for r in factor_refs]))
                coeff_ref[at] = product(factor, split(coeff_ref[at]))
            for at in blocks:
                change = product(refl(at), split(coeff_ref[at]))
                work_ref[rows(at), :] = source[rows(at), :] - change

        run(step, x_ref, range(count), 0, (0, count - 1))
        top_ref[...] = work_ref[:strip, :]
        low_ref[...] = work_ref[height - strip :, :]
        run(step + 1, work_ref, range(count - 1), strip, ())

    args = near(kinds, x, *coeffs, *refls, *factors)
    return pl.pallas_call(
        body,
        out_shape=[shape(height, width)] + [shape(strip, width)] * 2,
        in_specs=[VMEM] * len(args),
        out_specs=[VMEM] * 3,
        scratch_shapes=[pltpu.VMEM((count, strip, width), F32)],
        name="middle",
        compiler_params=LEAN,
    )(*args)


def store(work, strip):
    height, width = work.shape

    def body(work_ref, out_ref, sem):
        inner = pl.ds(strip, height - 2 * strip)
        copy = pltpu.make_async_copy(work_ref.at[inner, :], out_ref.at[inner, :], sem)
        copy.start()
        copy.wait()

    return pl.pallas_call(
        body,
        out_shape=jax.ShapeDtypeStruct((height, width), F32),
        in_specs=[VMEM],
        out_specs=ANY,
        scratch_shapes=[pltpu.SemaphoreType.DMA],
        name="store",
        compiler_params=LEAN,
    )(*near(work))


def prepare(refls, factors, behind, kinds, step, strips, projs):
    strip, width = strips[0].shape
    height, count = refls[0].shape[1], factors[0].shape[1]
    n = len(refls)

    def body(kinds_ref, top_ref, low_ref, even_ref, odd_ref, *refs):
        refl_refs, factor_refs = apart(refs[:n]), apart(refs[n : 2 * n])
        behind_refs, refs = apart(refs[2 * n : 3 * n]), refs[3 * n :]
        rests, highs, lows = refs[:2], refs[2:4], refs[4:]
        row, last = lax.axis_index("row"), lax.axis_size("row") - 1
        projs = ordered(even_ref[...], odd_ref[...])

        def weight(start, ends, present):
            refl = pick(kinds_ref, step + 1, [r[start : start + strip, :] for r in refl_refs])
            value = product(split(refl), split(pick(kinds_ref, step + 1, ends)))
            return jnp.where(present, value, jnp.zeros_like(value))

        top = weight(0, [r[...] for r in behind_refs], row > 0)
        low = weight(height - strip, [r[count - 1] for r in factor_refs], row < last)
        even, odd = ordered(top, low)
        highs[0][...], lows[0][...] = split(even)
        highs[1][...], lows[1][...] = split(odd)
        top = top_ref[...] - product(split(top), split(projs[0]))
        low = low_ref[...] - product(split(low), split(projs[1]))
        rests[0][...], rests[1][...] = ordered(top, low)

    rest, half = shape(strip, width), shape(strip, strip, dtype=BF16)
    return vmem_call(
        body,
        [rest, rest, half, half, half, half],
        "prepare",
        *(kinds, *strips, *projs, *refls, *factors, *behind),
    )


def finish(out, prepared, gots):
    height, width = out.shape
    strip = gots[0].shape[0]

    def body(*refs):
        rests, highs, lows, gots = refs[:2], refs[2:4], refs[4:6], refs[6:8]
        out_ref, new_ref, sem = refs[9:]
        row, last = lax.axis_index("row"), lax.axis_size("row") - 1
        copies = []
        for at in range(2):
            top = is_top(at == 1)
            present = jnp.where(top, row > 0, row < last)
            other = jnp.where(present, gots[at][...], jnp.zeros_like(gots[at]))
            weight = highs[at][...], lows[at][...]
            new_ref[at] = rests[at][...] - product(weight, split(other))
            start = pl.multiple_of(jnp.where(top, 0, height - strip), strip)
            rows = out_ref.at[pl.ds(start, strip), :]
            copies.append(pltpu.make_async_copy(new_ref.at[at], rows, sem.at[at]))
            copies[-1].start()
        for copy in copies:
            copy.wait()

    return pl.pallas_call(
        body,
        out_shape=jax.ShapeDtypeStruct((height, width), F32),
        in_specs=[VMEM] * 8 + [ANY],
        out_specs=ANY,
        scratch_shapes=[pltpu.VMEM((2, strip, width), F32), pltpu.SemaphoreType.DMA((2,))],
        input_output_aliases={8: 0},
        name="finish",
        compiler_params=LEAN,
    )(*near(*prepared, *gots), out)


def local(vectors, reflectors, tfactors, plan):
    groups, strip = plan.shape[0], reflectors.shape[2]
    rows, columns = lax.axis_size("row"), lax.axis_size("col")

    def around(block, shift):
        return lax.ppermute(block, "col", [(c, (c + shift) % columns) for c in range(columns)])

    def trade(block, odd_round):
        route = []
        for row in range(rows):
            for col in range(columns):
                there = row + 1 if (row % 2 == 1) == odd_round else row - 1
                there = (there, col) if 0 <= there < rows else (row, (col + 1) % columns)
                route.append((row * columns + col, there[0] * columns + there[1]))
        return lax.ppermute(block, ("row", "col"), route)

    def everyone(piece):
        return [piece, *(around(piece, shift) for shift in range(1, columns))]

    refls, factors = everyone(reflectors), everyone(tfactors)
    plan = plan.reshape(1, groups)
    mark = entry(plan, vectors, reflectors, tfactors)
    kinds, end = tables(mark, tfactors, plan, columns)
    behind = lax.ppermute(end, "row", [(r, (r + 1) % rows) for r in range(rows)])
    current, behinds = vectors, None
    for step in range(0, groups, 2):
        coeffs, projs, gots = [], [], []
        for odd_round in (False, True):
            coeff, proj = edge(current, refls, factors, kinds, step, odd_round)
            coeffs.append(coeff)
            projs.append(proj)
            gots.append(trade(proj, odd_round))
        work, *strips = middle(current, refls, factors, kinds, step, coeffs)
        if behinds is None:
            behind, strips[0] = lax.optimization_barrier((behind, strips[0]))
            behinds = everyone(behind)
        out = store(work, strip)
        prepared = prepare(refls, factors, behinds, kinds, step, strips, projs)
        current = finish(out, prepared, gots)
    return current


def solution(mesh):
    return jax.shard_map(
        local,
        mesh=mesh,
        in_specs=(P("row", "col"), P("col", "row", None), P("col", "row", None, None), P()),
        out_specs=P("row", "col"),
        check_vma=False,
    )
```

```python
import jax
import jax.numpy as jnp
from jax import lax
from jax.experimental import pallas as pl
from jax.experimental.pallas import tpu as pltpu
from jax.sharding import PartitionSpec as P

F32 = jnp.float32
BF16 = jnp.bfloat16
LANES = 128
VMEM = pl.BlockSpec(memory_space=pltpu.VMEM)
HBM = pl.BlockSpec(memory_space=pltpu.HBM)
ANY = pl.BlockSpec(memory_space=pl.ANY)
LEAN = pltpu.CompilerParams(vmem_limit_bytes=8 << 20)


def split(a):
    high = a.astype(BF16)
    return high, (a - high.astype(F32)).astype(BF16)


def dot(a, b, over):
    return lax.dot_general(a, b, (((over,), (0,)), ((), ())), preferred_element_type=F32)


def product(a, b, over=1):
    (ah, al), (bh, bl) = a, b
    if ah.shape[over] > LANES:
        both = dot(jnp.concatenate([ah, al], 1 - over), bh, over)
        rows = ah.shape[1 - over]
        return both[:rows] + (both[rows:] + dot(ah, bl, over))
    return dot(jnp.concatenate([ah, al], over), jnp.concatenate([bh, bh], 0), over) + dot(ah, bl, over)


def pick(kinds, step, pieces):
    value = pieces[0]
    for at, piece in enumerate(pieces[1:], 1):
        mask = jnp.broadcast_to(kinds[step : step + 1, :], value.shape) == at
        value = jnp.where(mask, piece, value)
    return value


def shape(*dims, dtype=F32):
    return pltpu.VMEM(dims, dtype)


def near(*values, space=pltpu.VMEM):
    return [pltpu.with_memory_space_constraint(value, space) for value in values]


def vmem_call(body, outs, name, *args):
    return pl.pallas_call(
        body,
        out_shape=outs,
        in_specs=[VMEM] * len(args),
        out_specs=[VMEM] * len(outs),
        name=name,
        compiler_params=LEAN,
    )(*near(*args))


def entry(*arrays):
    lanes = (8, LANES)

    def body(*refs):
        refs[-1][...] = jnp.zeros(lanes, F32)

    return pl.pallas_call(
        body,
        out_shape=shape(*lanes),
        in_specs=[HBM] * len(arrays),
        out_specs=VMEM,
        name="entry",
        compiler_params=LEAN,
    )(*near(*arrays, space=pltpu.HBM))


def tables(mark, tfactors, plan, columns):
    held, count, lanes = tfactors.shape[:3]
    groups = plan.shape[1]

    def body(_, plan_ref, f_ref, kinds_ref, end_ref):
        end_ref[...] = f_ref[:, count - 1]
        me = lax.axis_index("col")
        kinds_ref[...] = jnp.zeros_like(kinds_ref)
        for step in range(groups):
            group = jnp.broadcast_to(plan_ref[:, step : step + 1], (1, lanes))
            home = group // held if held > 1 else group
            gap = me - home
            gap = jnp.where(gap < 0, gap + columns, gap)
            kinds_ref[step : step + 1, :] = gap * held + (group - home * held)

    table = shape(-(-groups // 8) * 8, lanes, dtype=jnp.int32)
    return vmem_call(body, [table, shape(held, lanes, lanes)], "tables", mark, plan, tfactors)


def is_top(odd_round):
    return (lax.axis_index("row") % 2 == 1) != odd_round


def ordered(top, low):
    first = is_top(False)
    return jnp.where(first, top, low), jnp.where(first, low, top)


def apart(pieces):
    return [piece.at[slot] for piece in pieces for slot in range(piece.shape[0])]


def edge(x, refls, factors, kinds, step, odd_round):
    width, strip = x.shape[1], refls[0].shape[2]
    block = 2 * strip
    count = factors[0].shape[1]
    n = len(refls)

    def body(kinds_ref, x_ref, *refs):
        refl_refs, factor_refs = apart(refs[:n]), apart(refs[n : 2 * n])
        coeff_ref, proj_ref = refs[-2:]

        def work(at, outer):
            start = at * block
            rows, side = slice(start, start + block), slice(start + outer, start + outer + strip)
            first = split(pick(kinds_ref, step, [r[rows, :] for r in refl_refs]))
            second = split(pick(kinds_ref, step + 1, [r[side, :] for r in refl_refs]))
            high, low = split(x_ref[rows, :])
            cross = product(second, [v[outer : outer + strip] for v in first], over=0)
            blank = jnp.zeros((strip, strip), BF16)
            second = [jnp.concatenate([v, blank] if outer == 0 else [blank, v], 0) for v in second]
            all_high = dot(jnp.concatenate([*first, *second], 1), high, 0)
            all_low = dot(jnp.concatenate([first[0], second[0]], 1), low, 0)
            factor = pick(kinds_ref, step, [r[at] for r in factor_refs])
            weight = product(split(cross), split(factor))
            parts = [all_high[i * strip : (i + 1) * strip] for i in range(4)]
            coeff = parts[0] + (parts[1] + all_low[:strip])
            coeff_ref[...] = coeff
            rest = product(split(weight), split(coeff))
            proj_ref[...] = parts[2] + (parts[3] + all_low[strip:]) - rest

        top = is_top(odd_round)
        pl.when(top)(lambda: work(0, 0))
        pl.when(jnp.logical_not(top))(lambda: work(count - 1, strip))

    args = (kinds, x, *refls, *factors)
    return vmem_call(body, [shape(strip, width)] * 2, "edge", *args)


def middle(x, refls, factors, kinds, step, coeffs):
    height, width = x.shape
    strip = refls[0].shape[2]
    block = 2 * strip
    count = height // block
    n = len(refls)

    def body(kinds_ref, x_ref, even_coeff, odd_coeff, *refs):
        refl_refs, factor_refs = apart(refs[:n]), apart(refs[n : 2 * n])
        work_ref, top_ref, low_ref, coeff_ref = refs[2 * n :]
        coeff_ref[0], coeff_ref[count - 1] = ordered(even_coeff[...], odd_coeff[...])

        def run(step, source, blocks, offset, known):
            def rows(at):
                return slice(at * block + offset, (at + 1) * block + offset)

            def refl(at):
                return split(pick(kinds_ref, step, [r[rows(at), :] for r in refl_refs]))

            for at in blocks:
                if at not in known:
                    coeff_ref[at] = product(refl(at), split(source[rows(at), :]), over=0)
            for at in blocks:
                factor = split(pick(kinds_ref, step, [r[at] for r in factor_refs]))
                coeff_ref[at] = product(factor, split(coeff_ref[at]))
            for at in blocks:
                change = product(refl(at), split(coeff_ref[at]))
                work_ref[rows(at), :] = source[rows(at), :] - change

        run(step, x_ref, range(count), 0, (0, count - 1))
        top_ref[...] = work_ref[:strip, :]
        low_ref[...] = work_ref[height - strip :, :]
        run(step + 1, work_ref, range(count - 1), strip, ())

    args = near(kinds, x, *coeffs, *refls, *factors)
    return pl.pallas_call(
        body,
        out_shape=[shape(height, width)] + [shape(strip, width)] * 2,
        in_specs=[VMEM] * len(args),
        out_specs=[VMEM] * 3,
        scratch_shapes=[pltpu.VMEM((count, strip, width), F32)],
        name="middle",
        compiler_params=LEAN,
    )(*args)


def store(work, strip):
    height, width = work.shape

    def body(work_ref, out_ref, sem):
        inner = pl.ds(strip, height - 2 * strip)
        copy = pltpu.make_async_copy(work_ref.at[inner, :], out_ref.at[inner, :], sem)
        copy.start()
        copy.wait()

    return pl.pallas_call(
        body,
        out_shape=jax.ShapeDtypeStruct((height, width), F32),
        in_specs=[VMEM],
        out_specs=ANY,
        scratch_shapes=[pltpu.SemaphoreType.DMA],
        name="store",
        compiler_params=LEAN,
    )(*near(work))


def prepare(refls, factors, behind, kinds, step, strips, projs):
    strip, width = strips[0].shape
    height, count = refls[0].shape[1], factors[0].shape[1]
    n = len(refls)

    def body(kinds_ref, top_ref, low_ref, even_ref, odd_ref, *refs):
        refl_refs, factor_refs = apart(refs[:n]), apart(refs[n : 2 * n])
        behind_refs, refs = apart(refs[2 * n : 3 * n]), refs[3 * n :]
        rests, highs, lows = refs[:2], refs[2:4], refs[4:]
        row, last = lax.axis_index("row"), lax.axis_size("row") - 1
        projs = ordered(even_ref[...], odd_ref[...])

        def weight(start, ends, present):
            refl = pick(kinds_ref, step + 1, [r[start : start + strip, :] for r in refl_refs])
            value = product(split(refl), split(pick(kinds_ref, step + 1, ends)))
            return jnp.where(present, value, jnp.zeros_like(value))

        top = weight(0, [r[...] for r in behind_refs], row > 0)
        low = weight(height - strip, [r[count - 1] for r in factor_refs], row < last)
        even, odd = ordered(top, low)
        highs[0][...], lows[0][...] = split(even)
        highs[1][...], lows[1][...] = split(odd)
        top = top_ref[...] - product(split(top), split(projs[0]))
        low = low_ref[...] - product(split(low), split(projs[1]))
        rests[0][...], rests[1][...] = ordered(top, low)

    rest, half = shape(strip, width), shape(strip, strip, dtype=BF16)
    return vmem_call(
        body,
        [rest, rest, half, half, half, half],
        "prepare",
        *(kinds, *strips, *projs, *refls, *factors, *behind),
    )


def finish(out, prepared, gots):
    height, width = out.shape
    strip = gots[0].shape[0]

    def body(*refs):
        rests, highs, lows, gots = refs[:2], refs[2:4], refs[4:6], refs[6:8]
        out_ref, new_ref, sem = refs[9:]
        row, last = lax.axis_index("row"), lax.axis_size("row") - 1
        copies = []
        for at in range(2):
            top = is_top(at == 1)
            present = jnp.where(top, row > 0, row < last)
            other = jnp.where(present, gots[at][...], jnp.zeros_like(gots[at]))
            weight = highs[at][...], lows[at][...]
            new_ref[at] = rests[at][...] - product(weight, split(other))
            start = pl.multiple_of(jnp.where(top, 0, height - strip), strip)
            rows = out_ref.at[pl.ds(start, strip), :]
            copies.append(pltpu.make_async_copy(new_ref.at[at], rows, sem.at[at]))
            copies[-1].start()
        for copy in copies:
            copy.wait()

    return pl.pallas_call(
        body,
        out_shape=jax.ShapeDtypeStruct((height, width), F32),
        in_specs=[VMEM] * 8 + [ANY],
        out_specs=ANY,
        scratch_shapes=[pltpu.VMEM((2, strip, width), F32), pltpu.SemaphoreType.DMA((2,))],
        input_output_aliases={8: 0},
        name="finish",
        compiler_params=LEAN,
    )(*near(*prepared, *gots), out)


def local(vectors, reflectors, tfactors, plan):
    groups, strip = plan.shape[0], reflectors.shape[2]
    rows, columns = lax.axis_size("row"), lax.axis_size("col")

    def around(block, shift):
        return lax.ppermute(block, "col", [(c, (c + shift) % columns) for c in range(columns)])

    def trade(block, odd_round):
        route = []
        for row in range(rows):
            for col in range(columns):
                there = row + 1 if (row % 2 == 1) == odd_round else row - 1
                there = (there, col) if 0 <= there < rows else (row, (col + 1) % columns)
                route.append((row * columns + col, there[0] * columns + there[1]))
        return lax.ppermute(block, ("row", "col"), route)

    def everyone(piece, sent):
        return [piece, *(around(sent, shift) for shift in range(1, columns))]

    plan = plan.reshape(1, groups)
    mark = entry(plan, vectors, reflectors, tfactors)
    later, mark = lax.optimization_barrier((tfactors, mark))
    refls, factors = everyone(reflectors, reflectors), everyone(tfactors, later)
    kinds, end = tables(mark, tfactors, plan, columns)
    behind = lax.ppermute(end, "row", [(r, (r + 1) % rows) for r in range(rows)])
    current, behinds = vectors, None
    for step in range(0, groups, 2):
        coeffs, projs, gots = [], [], []
        for odd_round in (False, True):
            coeff, proj = edge(current, refls, factors, kinds, step, odd_round)
            coeffs.append(coeff)
            projs.append(proj)
            gots.append(trade(proj, odd_round))
        work, *strips = middle(current, refls, factors, kinds, step, coeffs)
        if behinds is None:
            behind, strips[0] = lax.optimization_barrier((behind, strips[0]))
            behinds = everyone(behind, behind)
        out = store(work, strip)
        prepared = prepare(refls, factors, behinds, kinds, step, strips, projs)
        current = finish(out, prepared, gots)
    return current


def solution(mesh):
    return jax.shard_map(
        local,
        mesh=mesh,
        in_specs=(P("row", "col"), P("col", "row", None), P("col", "row", None, None), P()),
        out_specs=P("row", "col"),
        check_vma=False,
    )
```

```python
import jax
import jax.numpy as jnp
from jax import lax
from jax.experimental import pallas as pl
from jax.experimental.pallas import tpu as pltpu
from jax.sharding import PartitionSpec as P

F32 = jnp.float32
BF16 = jnp.bfloat16
LANES = 128
VMEM = pl.BlockSpec(memory_space=pltpu.VMEM)
HBM = pl.BlockSpec(memory_space=pltpu.HBM)
ANY = pl.BlockSpec(memory_space=pl.ANY)
LEAN = pltpu.CompilerParams(vmem_limit_bytes=8 << 20)


def split(a):
    high = a.astype(BF16)
    return high, (a - high.astype(F32)).astype(BF16)


def dot(a, b, over):
    return lax.dot_general(a, b, (((over,), (0,)), ((), ())), preferred_element_type=F32)


def product(a, b, over=1):
    (ah, al), (bh, bl) = a, b
    if ah.shape[over] > LANES:
        both = dot(jnp.concatenate([ah, al], 1 - over), bh, over)
        rows = ah.shape[1 - over]
        return both[:rows] + (both[rows:] + dot(ah, bl, over))
    return dot(jnp.concatenate([ah, al], over), jnp.concatenate([bh, bh], 0), over) + dot(ah, bl, over)


def pick(kinds, step, pieces):
    value = pieces[0]
    for at, piece in enumerate(pieces[1:], 1):
        mask = jnp.broadcast_to(kinds[step : step + 1, :], value.shape) == at
        value = jnp.where(mask, piece, value)
    return value


def shape(*dims, dtype=F32):
    return pltpu.VMEM(dims, dtype)


def near(*values, space=pltpu.VMEM):
    return [pltpu.with_memory_space_constraint(value, space) for value in values]


def vmem_call(body, outs, name, *args):
    return pl.pallas_call(
        body,
        out_shape=outs,
        in_specs=[VMEM] * len(args),
        out_specs=[VMEM] * len(outs),
        name=name,
        compiler_params=LEAN,
    )(*near(*args))


def entry(*arrays, after=()):
    lanes = (8, LANES)

    def body(*refs):
        refs[-1][...] = jnp.zeros(lanes, F32)

    return pl.pallas_call(
        body,
        out_shape=shape(*lanes),
        in_specs=[VMEM] * len(after) + [HBM] * len(arrays),
        out_specs=VMEM,
        name="entry",
        compiler_params=LEAN,
    )(*near(*after), *near(*arrays, space=pltpu.HBM))


def tables(mark, tfactors, plan, columns):
    held, count, lanes = tfactors.shape[:3]
    groups = plan.shape[1]

    def body(_, plan_ref, f_ref, kinds_ref, end_ref):
        end_ref[...] = f_ref[:, count - 1]
        me = lax.axis_index("col")
        kinds_ref[...] = jnp.zeros_like(kinds_ref)
        for step in range(groups):
            group = jnp.broadcast_to(plan_ref[:, step : step + 1], (1, lanes))
            home = group // held if held > 1 else group
            gap = me - home
            gap = jnp.where(gap < 0, gap + columns, gap)
            kinds_ref[step : step + 1, :] = gap * held + (group - home * held)

    table = shape(-(-groups // 8) * 8, lanes, dtype=jnp.int32)
    return vmem_call(body, [table, shape(held, lanes, lanes)], "tables", mark, plan, tfactors)


def is_top(odd_round):
    return (lax.axis_index("row") % 2 == 1) != odd_round


def ordered(top, low):
    first = is_top(False)
    return jnp.where(first, top, low), jnp.where(first, low, top)


def apart(pieces):
    return [piece.at[slot] for piece in pieces for slot in range(piece.shape[0])]


def edge(x, refls, factors, kinds, step, odd_round):
    width, strip = x.shape[1], refls[0].shape[2]
    block = 2 * strip
    count = factors[0].shape[1]
    n = len(refls)

    def body(kinds_ref, x_ref, *refs):
        refl_refs, factor_refs = apart(refs[:n]), apart(refs[n : 2 * n])
        coeff_ref, proj_ref = refs[-2:]

        def work(at, outer):
            start = at * block
            rows, side = slice(start, start + block), slice(start + outer, start + outer + strip)
            first = split(pick(kinds_ref, step, [r[rows, :] for r in refl_refs]))
            second = split(pick(kinds_ref, step + 1, [r[side, :] for r in refl_refs]))
            high, low = split(x_ref[rows, :])
            cross = product(second, [v[outer : outer + strip] for v in first], over=0)
            blank = jnp.zeros((strip, strip), BF16)
            second = [jnp.concatenate([v, blank] if outer == 0 else [blank, v], 0) for v in second]
            all_high = dot(jnp.concatenate([*first, *second], 1), high, 0)
            all_low = dot(jnp.concatenate([first[0], second[0]], 1), low, 0)
            factor = pick(kinds_ref, step, [r[at] for r in factor_refs])
            weight = product(split(cross), split(factor))
            parts = [all_high[i * strip : (i + 1) * strip] for i in range(4)]
            coeff = parts[0] + (parts[1] + all_low[:strip])
            coeff_ref[...] = coeff
            rest = product(split(weight), split(coeff))
            proj_ref[...] = parts[2] + (parts[3] + all_low[strip:]) - rest

        top = is_top(odd_round)
        pl.when(top)(lambda: work(0, 0))
        pl.when(jnp.logical_not(top))(lambda: work(count - 1, strip))

    args = (kinds, x, *refls, *factors)
    return vmem_call(body, [shape(strip, width)] * 2, "edge", *args)


def middle(x, refls, factors, kinds, step, coeffs):
    height, width = x.shape
    strip = refls[0].shape[2]
    block = 2 * strip
    count = height // block
    n = len(refls)

    def body(kinds_ref, x_ref, even_coeff, odd_coeff, *refs):
        refl_refs, factor_refs = apart(refs[:n]), apart(refs[n : 2 * n])
        work_ref, top_ref, low_ref, coeff_ref = refs[2 * n :]
        coeff_ref[0], coeff_ref[count - 1] = ordered(even_coeff[...], odd_coeff[...])

        def run(step, source, blocks, offset, known):
            def rows(at):
                return slice(at * block + offset, (at + 1) * block + offset)

            def refl(at):
                return split(pick(kinds_ref, step, [r[rows(at), :] for r in refl_refs]))

            for at in blocks:
                if at not in known:
                    coeff_ref[at] = product(refl(at), split(source[rows(at), :]), over=0)
            for at in blocks:
                factor = split(pick(kinds_ref, step, [r[at] for r in factor_refs]))
                coeff_ref[at] = product(factor, split(coeff_ref[at]))
            for at in blocks:
                change = product(refl(at), split(coeff_ref[at]))
                work_ref[rows(at), :] = source[rows(at), :] - change

        run(step, x_ref, range(count), 0, (0, count - 1))
        top_ref[...] = work_ref[:strip, :]
        low_ref[...] = work_ref[height - strip :, :]
        run(step + 1, work_ref, range(count - 1), strip, ())

    args = near(kinds, x, *coeffs, *refls, *factors)
    return pl.pallas_call(
        body,
        out_shape=[shape(height, width)] + [shape(strip, width)] * 2,
        in_specs=[VMEM] * len(args),
        out_specs=[VMEM] * 3,
        scratch_shapes=[pltpu.VMEM((count, strip, width), F32)],
        name="middle",
        compiler_params=LEAN,
    )(*args)


def store(work, strip):
    height, width = work.shape

    def body(work_ref, out_ref, sem):
        inner = pl.ds(strip, height - 2 * strip)
        copy = pltpu.make_async_copy(work_ref.at[inner, :], out_ref.at[inner, :], sem)
        copy.start()
        copy.wait()

    return pl.pallas_call(
        body,
        out_shape=jax.ShapeDtypeStruct((height, width), F32),
        in_specs=[VMEM],
        out_specs=ANY,
        scratch_shapes=[pltpu.SemaphoreType.DMA],
        name="store",
        compiler_params=LEAN,
    )(*near(work))


def prepare(refls, factors, behind, kinds, step, strips, projs):
    strip, width = strips[0].shape
    height, count = refls[0].shape[1], factors[0].shape[1]
    n = len(refls)

    def body(kinds_ref, top_ref, low_ref, even_ref, odd_ref, *refs):
        refl_refs, factor_refs = apart(refs[:n]), apart(refs[n : 2 * n])
        behind_refs, refs = apart(refs[2 * n : 3 * n]), refs[3 * n :]
        rests, highs, lows = refs[:2], refs[2:4], refs[4:]
        row, last = lax.axis_index("row"), lax.axis_size("row") - 1
        projs = ordered(even_ref[...], odd_ref[...])

        def weight(start, ends, present):
            refl = pick(kinds_ref, step + 1, [r[start : start + strip, :] for r in refl_refs])
            value = product(split(refl), split(pick(kinds_ref, step + 1, ends)))
            return jnp.where(present, value, jnp.zeros_like(value))

        top = weight(0, [r[...] for r in behind_refs], row > 0)
        low = weight(height - strip, [r[count - 1] for r in factor_refs], row < last)
        even, odd = ordered(top, low)
        highs[0][...], lows[0][...] = split(even)
        highs[1][...], lows[1][...] = split(odd)
        top = top_ref[...] - product(split(top), split(projs[0]))
        low = low_ref[...] - product(split(low), split(projs[1]))
        rests[0][...], rests[1][...] = ordered(top, low)

    rest, half = shape(strip, width), shape(strip, strip, dtype=BF16)
    return vmem_call(
        body,
        [rest, rest, half, half, half, half],
        "prepare",
        *(kinds, *strips, *projs, *refls, *factors, *behind),
    )


def finish(out, prepared, gots):
    height, width = out.shape
    strip = gots[0].shape[0]

    def body(*refs):
        rests, highs, lows, gots = refs[:2], refs[2:4], refs[4:6], refs[6:8]
        out_ref, new_ref, sem = refs[9:]
        row, last = lax.axis_index("row"), lax.axis_size("row") - 1
        copies = []
        for at in range(2):
            top = is_top(at == 1)
            present = jnp.where(top, row > 0, row < last)
            other = jnp.where(present, gots[at][...], jnp.zeros_like(gots[at]))
            weight = highs[at][...], lows[at][...]
            new_ref[at] = rests[at][...] - product(weight, split(other))
            start = pl.multiple_of(jnp.where(top, 0, height - strip), strip)
            rows = out_ref.at[pl.ds(start, strip), :]
            copies.append(pltpu.make_async_copy(new_ref.at[at], rows, sem.at[at]))
            copies[-1].start()
        for copy in copies:
            copy.wait()

    return pl.pallas_call(
        body,
        out_shape=jax.ShapeDtypeStruct((height, width), F32),
        in_specs=[VMEM] * 8 + [ANY],
        out_specs=ANY,
        scratch_shapes=[pltpu.VMEM((2, strip, width), F32), pltpu.SemaphoreType.DMA((2,))],
        input_output_aliases={8: 0},
        name="finish",
        compiler_params=LEAN,
    )(*near(*prepared, *gots), out)


def local(vectors, reflectors, tfactors, plan):
    groups, strip = plan.shape[0], reflectors.shape[2]
    rows, columns = lax.axis_size("row"), lax.axis_size("col")

    def around(block, shift):
        return lax.ppermute(block, "col", [(c, (c + shift) % columns) for c in range(columns)])

    def trade(block, odd_round):
        route = []
        for row in range(rows):
            for col in range(columns):
                there = row + 1 if (row % 2 == 1) == odd_round else row - 1
                there = (there, col) if 0 <= there < rows else (row, (col + 1) % columns)
                route.append((row * columns + col, there[0] * columns + there[1]))
        return lax.ppermute(block, ("row", "col"), route)

    def everyone(piece, sent):
        return [piece, *(around(sent, shift) for shift in range(1, columns))]

    factors = everyone(tfactors, tfactors)
    plan = plan.reshape(1, groups)
    mark = entry(plan, tfactors)
    later, mark = lax.optimization_barrier((reflectors, mark))
    refls = everyone(reflectors, later)
    mark = entry(vectors, reflectors, after=(mark,))
    kinds, end = tables(mark, tfactors, plan, columns)
    behind = lax.ppermute(end, "row", [(r, (r + 1) % rows) for r in range(rows)])
    current, behinds = vectors, None
    for step in range(0, groups, 2):
        coeffs, projs, gots = [], [], []
        for odd_round in (False, True):
            coeff, proj = edge(current, refls, factors, kinds, step, odd_round)
            coeffs.append(coeff)
            projs.append(proj)
            gots.append(trade(proj, odd_round))
        work, *strips = middle(current, refls, factors, kinds, step, coeffs)
        if behinds is None:
            behind, strips[0] = lax.optimization_barrier((behind, strips[0]))
            behinds = everyone(behind, behind)
        out = store(work, strip)
        prepared = prepare(refls, factors, behinds, kinds, step, strips, projs)
        current = finish(out, prepared, gots)
    return current


def solution(mesh):
    return jax.shard_map(
        local,
        mesh=mesh,
        in_specs=(P("row", "col"), P("col", "row", None), P("col", "row", None, None), P()),
        out_specs=P("row", "col"),
        check_vma=False,
    )
```

```python
import jax
import jax.numpy as jnp
from jax import lax
from jax.experimental import pallas as pl
from jax.experimental.pallas import tpu as pltpu
from jax.sharding import PartitionSpec as P

F32 = jnp.float32
BF16 = jnp.bfloat16
LANES = 128
VMEM = pl.BlockSpec(memory_space=pltpu.VMEM)
HBM = pl.BlockSpec(memory_space=pltpu.HBM)
ANY = pl.BlockSpec(memory_space=pl.ANY)
LEAN = pltpu.CompilerParams(vmem_limit_bytes=8 << 20)


def split(a):
    high = a.astype(BF16)
    return high, (a - high.astype(F32)).astype(BF16)


def dot(a, b, over):
    return lax.dot_general(a, b, (((over,), (0,)), ((), ())), preferred_element_type=F32)


def product(a, b, over=1):
    (ah, al), (bh, bl) = a, b
    if ah.shape[over] > LANES:
        both = dot(jnp.concatenate([ah, al], 1 - over), bh, over)
        rows = ah.shape[1 - over]
        return both[:rows] + (both[rows:] + dot(ah, bl, over))
    return dot(jnp.concatenate([ah, al], over), jnp.concatenate([bh, bh], 0), over) + dot(ah, bl, over)


def pick(kinds, step, pieces):
    value = pieces[0]
    for at, piece in enumerate(pieces[1:], 1):
        mask = jnp.broadcast_to(kinds[step : step + 1, :], value.shape) == at
        value = jnp.where(mask, piece, value)
    return value


def shape(*dims, dtype=F32):
    return pltpu.VMEM(dims, dtype)


def near(*values, space=pltpu.VMEM):
    return [pltpu.with_memory_space_constraint(value, space) for value in values]


def vmem_call(body, outs, name, *args):
    return pl.pallas_call(
        body,
        out_shape=outs,
        in_specs=[VMEM] * len(args),
        out_specs=[VMEM] * len(outs),
        name=name,
        compiler_params=LEAN,
    )(*near(*args))


def entry(*arrays, after=()):
    lanes = (8, LANES)

    def body(*refs):
        refs[-1][...] = jnp.zeros(lanes, F32)

    return pl.pallas_call(
        body,
        out_shape=shape(*lanes),
        in_specs=[VMEM] * len(after) + [HBM] * len(arrays),
        out_specs=VMEM,
        name="entry",
        compiler_params=LEAN,
    )(*near(*after), *near(*arrays, space=pltpu.HBM))


def fold(f):
    size = f.shape[1]
    part = size // 4
    lane = lax.broadcasted_iota(jnp.int32, (part, size), 1)
    rows = [f[at * part : (at + 1) * part] for at in range(4)]
    mixed = jnp.where(lane < part, pltpu.roll(rows[3], part, 1), rows[1])
    half = part // 2
    halves = jnp.where(lane[:half] < 2 * part, pltpu.roll(rows[2][:half], 2 * part, 1), rows[2][half:])
    return jnp.concatenate([rows[0], mixed, halves], 0)


def unfold(f):
    size = f.shape[1]
    part = size // 4
    half = part // 2
    lane = lax.broadcasted_iota(jnp.int32, (part, size), 1)
    mixed, halves = f[part : 2 * part], f[2 * part :]
    second = jnp.where(lane < part, 0.0, mixed)
    fourth = jnp.where(lane < 3 * part, 0.0, pltpu.roll(mixed, 3 * part, 1))
    third = [jnp.where(lane[:half] < 2 * part, 0.0, v) for v in (pltpu.roll(halves, 2 * part, 1), halves)]
    return jnp.concatenate([f[:part], second, *third, fourth], 0)


def tables(mark, tfactors, plan, columns):
    held, count, lanes = tfactors.shape[:3]
    groups = plan.shape[1]

    def body(_, plan_ref, f_ref, kinds_ref, end_ref):
        for slot in range(held):
            end_ref[slot] = fold(f_ref[slot, count - 1])
        me = lax.axis_index("col")
        kinds_ref[...] = jnp.zeros_like(kinds_ref)
        for step in range(groups):
            group = jnp.broadcast_to(plan_ref[:, step : step + 1], (1, lanes))
            home = group // held if held > 1 else group
            gap = me - home
            gap = jnp.where(gap < 0, gap + columns, gap)
            kinds_ref[step : step + 1, :] = gap * held + (group - home * held)

    table = shape(-(-groups // 8) * 8, lanes, dtype=jnp.int32)
    folded = shape(held, 5 * lanes // 8, lanes)
    return vmem_call(body, [table, folded], "tables", mark, plan, tfactors)


def is_top(odd_round):
    return (lax.axis_index("row") % 2 == 1) != odd_round


def ordered(top, low):
    first = is_top(False)
    return jnp.where(first, top, low), jnp.where(first, low, top)


def apart(pieces):
    return [piece.at[slot] for piece in pieces for slot in range(piece.shape[0])]


def edge(x, refls, factors, kinds, step, odd_round):
    width, strip = x.shape[1], refls[0].shape[2]
    block = 2 * strip
    count = factors[0].shape[1]
    n = len(refls)

    def body(kinds_ref, x_ref, *refs):
        refl_refs, factor_refs = apart(refs[:n]), apart(refs[n : 2 * n])
        coeff_ref, proj_ref = refs[-2:]

        def work(at, outer):
            start = at * block
            rows, side = slice(start, start + block), slice(start + outer, start + outer + strip)
            first = split(pick(kinds_ref, step, [r[rows, :] for r in refl_refs]))
            second = split(pick(kinds_ref, step + 1, [r[side, :] for r in refl_refs]))
            high, low = split(x_ref[rows, :])
            cross = product(second, [v[outer : outer + strip] for v in first], over=0)
            blank = jnp.zeros((strip, strip), BF16)
            second = [jnp.concatenate([v, blank] if outer == 0 else [blank, v], 0) for v in second]
            all_high = dot(jnp.concatenate([*first, *second], 1), high, 0)
            all_low = dot(jnp.concatenate([first[0], second[0]], 1), low, 0)
            factor = pick(kinds_ref, step, [r[at] for r in factor_refs])
            weight = product(split(cross), split(factor))
            parts = [all_high[i * strip : (i + 1) * strip] for i in range(4)]
            coeff = parts[0] + (parts[1] + all_low[:strip])
            coeff_ref[...] = coeff
            rest = product(split(weight), split(coeff))
            proj_ref[...] = parts[2] + (parts[3] + all_low[strip:]) - rest

        top = is_top(odd_round)
        pl.when(top)(lambda: work(0, 0))
        pl.when(jnp.logical_not(top))(lambda: work(count - 1, strip))

    args = (kinds, x, *refls, *factors)
    return vmem_call(body, [shape(strip, width)] * 2, "edge", *args)


def middle(x, refls, factors, kinds, step, coeffs):
    height, width = x.shape
    strip = refls[0].shape[2]
    block = 2 * strip
    count = height // block
    n = len(refls)

    def body(kinds_ref, x_ref, even_coeff, odd_coeff, *refs):
        refl_refs, factor_refs = apart(refs[:n]), apart(refs[n : 2 * n])
        work_ref, top_ref, low_ref, coeff_ref = refs[2 * n :]
        coeff_ref[0], coeff_ref[count - 1] = ordered(even_coeff[...], odd_coeff[...])

        def run(step, source, blocks, offset, known):
            def rows(at):
                return slice(at * block + offset, (at + 1) * block + offset)

            def refl(at):
                return split(pick(kinds_ref, step, [r[rows(at), :] for r in refl_refs]))

            for at in blocks:
                if at not in known:
                    coeff_ref[at] = product(refl(at), split(source[rows(at), :]), over=0)
            for at in blocks:
                factor = split(pick(kinds_ref, step, [r[at] for r in factor_refs]))
                coeff_ref[at] = product(factor, split(coeff_ref[at]))
            for at in blocks:
                change = product(refl(at), split(coeff_ref[at]))
                work_ref[rows(at), :] = source[rows(at), :] - change

        run(step, x_ref, range(count), 0, (0, count - 1))
        top_ref[...] = work_ref[:strip, :]
        low_ref[...] = work_ref[height - strip :, :]
        run(step + 1, work_ref, range(count - 1), strip, ())

    args = near(kinds, x, *coeffs, *refls, *factors)
    return pl.pallas_call(
        body,
        out_shape=[shape(height, width)] + [shape(strip, width)] * 2,
        in_specs=[VMEM] * len(args),
        out_specs=[VMEM] * 3,
        scratch_shapes=[pltpu.VMEM((count, strip, width), F32)],
        name="middle",
        compiler_params=LEAN,
    )(*args)


def store(work, strip):
    height, width = work.shape

    def body(work_ref, out_ref, sem):
        inner = pl.ds(strip, height - 2 * strip)
        copy = pltpu.make_async_copy(work_ref.at[inner, :], out_ref.at[inner, :], sem)
        copy.start()
        copy.wait()

    return pl.pallas_call(
        body,
        out_shape=jax.ShapeDtypeStruct((height, width), F32),
        in_specs=[VMEM],
        out_specs=ANY,
        scratch_shapes=[pltpu.SemaphoreType.DMA],
        name="store",
        compiler_params=LEAN,
    )(*near(work))


def prepare(refls, factors, behind, kinds, step, strips, projs):
    strip, width = strips[0].shape
    height, count = refls[0].shape[1], factors[0].shape[1]
    n = len(refls)

    def body(kinds_ref, top_ref, low_ref, even_ref, odd_ref, *refs):
        refl_refs, factor_refs = apart(refs[:n]), apart(refs[n : 2 * n])
        behind_refs, refs = apart(refs[2 * n : 3 * n]), refs[3 * n :]
        rests, highs, lows = refs[:2], refs[2:4], refs[4:]
        row, last = lax.axis_index("row"), lax.axis_size("row") - 1
        projs = ordered(even_ref[...], odd_ref[...])

        def weight(start, factor, present):
            refl = pick(kinds_ref, step + 1, [r[start : start + strip, :] for r in refl_refs])
            value = product(split(refl), split(factor))
            return jnp.where(present, value, jnp.zeros_like(value))

        before = unfold(pick(kinds_ref, step + 1, [r[...] for r in behind_refs]))
        own = pick(kinds_ref, step + 1, [r[count - 1] for r in factor_refs])
        top = weight(0, before, row > 0)
        low = weight(height - strip, own, row < last)
        even, odd = ordered(top, low)
        highs[0][...], lows[0][...] = split(even)
        highs[1][...], lows[1][...] = split(odd)
        top = top_ref[...] - product(split(top), split(projs[0]))
        low = low_ref[...] - product(split(low), split(projs[1]))
        rests[0][...], rests[1][...] = ordered(top, low)

    rest, half = shape(strip, width), shape(strip, strip, dtype=BF16)
    return vmem_call(
        body,
        [rest, rest, half, half, half, half],
        "prepare",
        *(kinds, *strips, *projs, *refls, *factors, *behind),
    )


def finish(out, prepared, gots):
    height, width = out.shape
    strip = gots[0].shape[0]

    def body(*refs):
        rests, highs, lows, gots = refs[:2], refs[2:4], refs[4:6], refs[6:8]
        out_ref, new_ref, sem = refs[9:]
        row, last = lax.axis_index("row"), lax.axis_size("row") - 1
        copies = []
        for at in range(2):
            top = is_top(at == 1)
            present = jnp.where(top, row > 0, row < last)
            other = jnp.where(present, gots[at][...], jnp.zeros_like(gots[at]))
            weight = highs[at][...], lows[at][...]
            new_ref[at] = rests[at][...] - product(weight, split(other))
            start = pl.multiple_of(jnp.where(top, 0, height - strip), strip)
            rows = out_ref.at[pl.ds(start, strip), :]
            copies.append(pltpu.make_async_copy(new_ref.at[at], rows, sem.at[at]))
            copies[-1].start()
        for copy in copies:
            copy.wait()

    return pl.pallas_call(
        body,
        out_shape=jax.ShapeDtypeStruct((height, width), F32),
        in_specs=[VMEM] * 8 + [ANY],
        out_specs=ANY,
        scratch_shapes=[pltpu.VMEM((2, strip, width), F32), pltpu.SemaphoreType.DMA((2,))],
        input_output_aliases={8: 0},
        name="finish",
        compiler_params=LEAN,
    )(*near(*prepared, *gots), out)


def local(vectors, reflectors, tfactors, plan):
    groups, strip = plan.shape[0], reflectors.shape[2]
    rows, columns = lax.axis_size("row"), lax.axis_size("col")

    def around(block, shift):
        return lax.ppermute(block, "col", [(c, (c + shift) % columns) for c in range(columns)])

    def trade(block, odd_round):
        route = []
        for row in range(rows):
            for col in range(columns):
                there = row + 1 if (row % 2 == 1) == odd_round else row - 1
                there = (there, col) if 0 <= there < rows else (row, (col + 1) % columns)
                route.append((row * columns + col, there[0] * columns + there[1]))
        return lax.ppermute(block, ("row", "col"), route)

    def everyone(piece, sent):
        return [piece, *(around(sent, shift) for shift in range(1, columns))]

    factors = everyone(tfactors, tfactors)
    plan = plan.reshape(1, groups)
    mark = entry(plan, tfactors)
    later, mark = lax.optimization_barrier((reflectors, mark))
    refls = everyone(reflectors, later)
    mark = entry(vectors, reflectors, after=(mark,))
    kinds, end = tables(mark, tfactors, plan, columns)
    behind = lax.ppermute(end, "row", [(r, (r + 1) % rows) for r in range(rows)])
    current, behinds = vectors, None
    for step in range(0, groups, 2):
        coeffs, projs, gots = [], [], []
        for odd_round in (False, True):
            coeff, proj = edge(current, refls, factors, kinds, step, odd_round)
            coeffs.append(coeff)
            projs.append(proj)
            gots.append(trade(proj, odd_round))
        work, *strips = middle(current, refls, factors, kinds, step, coeffs)
        if behinds is None:
            behind, strips[0] = lax.optimization_barrier((behind, strips[0]))
            behinds = everyone(behind, behind)
        out = store(work, strip)
        prepared = prepare(refls, factors, behinds, kinds, step, strips, projs)
        current = finish(out, prepared, gots)
    return current


def solution(mesh):
    return jax.shard_map(
        local,
        mesh=mesh,
        in_specs=(P("row", "col"), P("col", "row", None), P("col", "row", None, None), P()),
        out_specs=P("row", "col"),
        check_vma=False,
    )
```

```python
import jax
import jax.numpy as jnp
from jax import lax
from jax.experimental import pallas as pl
from jax.experimental.pallas import tpu as pltpu
from jax.sharding import PartitionSpec as P


F32 = jnp.float32
BF16 = jnp.bfloat16
LANES = 128
VMEM = pl.BlockSpec(memory_space=pltpu.VMEM)
HBM = pl.BlockSpec(memory_space=pltpu.HBM)
ANY = pl.BlockSpec(memory_space=pl.ANY)
LEAN = pltpu.CompilerParams(vmem_limit_bytes=8 << 20)


def split(a):
    high = a.astype(BF16)
    return high, (a - high.astype(F32)).astype(BF16)


def dot(a, b, over):
    return lax.dot_general(a, b, (((over,), (0,)), ((), ())), preferred_element_type=F32)


def product(a, b, over=1):
    (ah, al), (bh, bl) = a, b
    if ah.shape[over] > LANES:
        both = dot(jnp.concatenate([ah, al], 1 - over), bh, over)
        rows = ah.shape[1 - over]
        return both[:rows] + (both[rows:] + dot(ah, bl, over))
    return dot(jnp.concatenate([ah, al], over), jnp.concatenate([bh, bh], 0), over) + dot(ah, bl, over)


def pick(kinds, step, pieces):
    value = pieces[0]
    for at, piece in enumerate(pieces[1:], 1):
        mask = jnp.broadcast_to(kinds[step : step + 1, :], value.shape) == at
        value = jnp.where(mask, piece, value)
    return value


def shape(*dims, dtype=F32):
    return pltpu.VMEM(dims, dtype)


def near(*values, space=pltpu.VMEM):
    return [pltpu.with_memory_space_constraint(value, space) for value in values]


def vmem_call(body, outs, *args):
    return pl.pallas_call(
        body, out_shape=outs, in_specs=[VMEM] * len(args), out_specs=[VMEM] * len(outs), compiler_params=LEAN
    )(*near(*args))


def entry(*arrays, after=()):
    lanes = (8, LANES)

    def body(*refs):
        refs[-1][...] = jnp.zeros(lanes, F32)

    return pl.pallas_call(
        body,
        out_shape=shape(*lanes),
        in_specs=[VMEM] * len(after) + [HBM] * len(arrays),
        out_specs=VMEM,
        name="entry",
        compiler_params=LEAN,
    )(*near(*after), *near(*arrays, space=pltpu.HBM))


def fold(f):
    size = f.shape[1]
    part = size // 4
    lane = lax.broadcasted_iota(jnp.int32, (part, size), 1)
    rows = [f[at * part : (at + 1) * part] for at in range(4)]
    mixed = jnp.where(lane < part, pltpu.roll(rows[3], part, 1), rows[1])
    half = part // 2
    halves = jnp.where(lane[:half] < 2 * part, pltpu.roll(rows[2][:half], 2 * part, 1), rows[2][half:])
    return jnp.concatenate([rows[0], mixed, halves], 0)


def unfold(f):
    size = f.shape[1]
    part = size // 4
    half = part // 2
    lane = lax.broadcasted_iota(jnp.int32, (part, size), 1)
    mixed, halves = f[part : 2 * part], f[2 * part :]
    second = jnp.where(lane < part, 0.0, mixed)
    fourth = jnp.where(lane < 3 * part, 0.0, pltpu.roll(mixed, 3 * part, 1))
    third = [jnp.where(lane[:half] < 2 * part, 0.0, v) for v in (pltpu.roll(halves, 2 * part, 1), halves)]
    return jnp.concatenate([f[:part], second, *third, fourth], 0)


def tables(mark, tfactors, plan, columns):
    held, count, lanes = tfactors.shape[:3]
    groups = plan.shape[1]

    def body(_, plan_ref, f_ref, kinds_ref, end_ref):
        for slot in range(held):
            end_ref[slot] = fold(f_ref[slot, count - 1])
        me = lax.axis_index("col")
        kinds_ref[...] = jnp.zeros_like(kinds_ref)
        for step in range(groups):
            group = jnp.broadcast_to(plan_ref[:, step : step + 1], (1, lanes))
            home = group // held if held > 1 else group
            gap = me - home
            gap = jnp.where(gap < 0, gap + columns, gap)
            kinds_ref[step : step + 1, :] = gap * held + (group - home * held)

    table = shape(-(-groups // 8) * 8, lanes, dtype=jnp.int32)
    folded = shape(held, 5 * lanes // 8, lanes)
    return vmem_call(body, [table, folded], mark, plan, tfactors)


def is_top(odd_round):
    return (lax.axis_index("row") % 2 == 1) != odd_round


def ordered(top, low):
    first = is_top(False)
    return jnp.where(first, top, low), jnp.where(first, low, top)


def apart(pieces):
    return [piece.at[slot] for piece in pieces for slot in range(piece.shape[0])]


def edge(x, refls, factors, kinds, step, odd_round):
    width, strip = x.shape[1], refls[0].shape[2]
    block = 2 * strip
    count = factors[0].shape[1]
    n = len(refls)

    def body(kinds_ref, x_ref, *refs):
        refl_refs, factor_refs = apart(refs[:n]), apart(refs[n : 2 * n])
        coeff_ref, proj_ref = refs[-2:]

        def work(at, outer):
            start = at * block
            rows, side = slice(start, start + block), slice(start + outer, start + outer + strip)
            first = split(pick(kinds_ref, step, [r[rows, :] for r in refl_refs]))
            second = split(pick(kinds_ref, step + 1, [r[side, :] for r in refl_refs]))
            high, low = split(x_ref[rows, :])
            cross = product(second, [v[outer : outer + strip] for v in first], over=0)
            blank = jnp.zeros((strip, strip), BF16)
            second = [jnp.concatenate([v, blank] if outer == 0 else [blank, v], 0) for v in second]
            all_high = dot(jnp.concatenate([*first, *second], 1), high, 0)
            all_low = dot(jnp.concatenate([first[0], second[0]], 1), low, 0)
            factor = pick(kinds_ref, step, [r[at] for r in factor_refs])
            weight = product(split(cross), split(factor))
            parts = [all_high[i * strip : (i + 1) * strip] for i in range(4)]
            coeff = parts[0] + (parts[1] + all_low[:strip])
            coeff_ref[...] = coeff
            rest = product(split(weight), split(coeff))
            proj_ref[...] = parts[2] + (parts[3] + all_low[strip:]) - rest

        top = is_top(odd_round)
        pl.when(top)(lambda: work(0, 0))
        pl.when(jnp.logical_not(top))(lambda: work(count - 1, strip))

    args = (kinds, x, *refls, *factors)
    return vmem_call(body, [shape(strip, width)] * 2, *args)


def middle(x, refls, factors, kinds, step, coeffs):
    height, width = x.shape
    strip = refls[0].shape[2]
    block = 2 * strip
    count = height // block
    n = len(refls)

    def body(kinds_ref, x_ref, even_coeff, odd_coeff, *refs):
        refl_refs, factor_refs = apart(refs[:n]), apart(refs[n : 2 * n])
        work_ref, top_ref, low_ref, coeff_ref = refs[2 * n :]
        coeff_ref[0], coeff_ref[count - 1] = ordered(even_coeff[...], odd_coeff[...])

        def run(step, source, blocks, offset, known):
            def rows(at):
                return slice(at * block + offset, (at + 1) * block + offset)

            def refl(at):
                return split(pick(kinds_ref, step, [r[rows(at), :] for r in refl_refs]))

            for at in blocks:
                if at not in known:
                    coeff_ref[at] = product(refl(at), split(source[rows(at), :]), over=0)
            for at in blocks:
                factor = split(pick(kinds_ref, step, [r[at] for r in factor_refs]))
                coeff_ref[at] = product(factor, split(coeff_ref[at]))
            for at in blocks:
                change = product(refl(at), split(coeff_ref[at]))
                work_ref[rows(at), :] = source[rows(at), :] - change

        run(step, x_ref, range(count), 0, (0, count - 1))
        top_ref[...] = work_ref[:strip, :]
        low_ref[...] = work_ref[height - strip :, :]
        run(step + 1, work_ref, range(count - 1), strip, ())

    args = near(kinds, x, *coeffs, *refls, *factors)
    return pl.pallas_call(
        body,
        out_shape=[shape(height, width)] + [shape(strip, width)] * 2,
        in_specs=[VMEM] * len(args),
        out_specs=[VMEM] * 3,
        scratch_shapes=[pltpu.VMEM((count, strip, width), F32)],
        name="middle",
        compiler_params=LEAN,
    )(*args)


def store(work, strip):
    height, width = work.shape

    def body(work_ref, out_ref, sem):
        inner = pl.ds(strip, height - 2 * strip)
        copy = pltpu.make_async_copy(work_ref.at[inner, :], out_ref.at[inner, :], sem)
        copy.start()
        copy.wait()

    return pl.pallas_call(
        body,
        out_shape=jax.ShapeDtypeStruct((height, width), F32),
        in_specs=[VMEM],
        out_specs=ANY,
        scratch_shapes=[pltpu.SemaphoreType.DMA],
        name="store",
        compiler_params=LEAN,
    )(*near(work))


def prepare(refls, factors, behind, kinds, step, strips, projs):
    strip, width = strips[0].shape
    height, count = refls[0].shape[1], factors[0].shape[1]
    n = len(refls)

    def body(kinds_ref, top_ref, low_ref, even_ref, odd_ref, *refs):
        refl_refs, factor_refs = apart(refs[:n]), apart(refs[n : 2 * n])
        behind_refs, refs = apart(refs[2 * n : 3 * n]), refs[3 * n :]
        rests, highs, lows = refs[:2], refs[2:4], refs[4:]
        row, last = lax.axis_index("row"), lax.axis_size("row") - 1
        projs = ordered(even_ref[...], odd_ref[...])

        def weight(start, factor, present):
            refl = pick(kinds_ref, step + 1, [r[start : start + strip, :] for r in refl_refs])
            value = product(split(refl), split(factor))
            return jnp.where(present, value, jnp.zeros_like(value))

        before = unfold(pick(kinds_ref, step + 1, [r[...] for r in behind_refs]))
        own = pick(kinds_ref, step + 1, [r[count - 1] for r in factor_refs])
        top = weight(0, before, row > 0)
        low = weight(height - strip, own, row < last)
        even, odd = ordered(top, low)
        highs[0][...], lows[0][...] = split(even)
        highs[1][...], lows[1][...] = split(odd)
        top = top_ref[...] - product(split(top), split(projs[0]))
        low = low_ref[...] - product(split(low), split(projs[1]))
        rests[0][...], rests[1][...] = ordered(top, low)

    rest, half = shape(strip, width), shape(strip, strip, dtype=BF16)
    return vmem_call(body, [rest, rest, half, half, half, half], *(kinds, *strips, *projs, *refls, *factors, *behind))


def finish(out, prepared, gots):
    height, width = out.shape
    strip = gots[0].shape[0]

    def body(*refs):
        rests, highs, lows, gots = refs[:2], refs[2:4], refs[4:6], refs[6:8]
        out_ref, new_ref, sem = refs[9:]
        row, last = lax.axis_index("row"), lax.axis_size("row") - 1
        copies = []
        for at in range(2):
            top = is_top(at == 1)
            present = jnp.where(top, row > 0, row < last)
            other = jnp.where(present, gots[at][...], jnp.zeros_like(gots[at]))
            weight = highs[at][...], lows[at][...]
            new_ref[at] = rests[at][...] - product(weight, split(other))
            start = pl.multiple_of(jnp.where(top, 0, height - strip), strip)
            rows = out_ref.at[pl.ds(start, strip), :]
            copies.append(pltpu.make_async_copy(new_ref.at[at], rows, sem.at[at]))
            copies[-1].start()
        for copy in copies:
            copy.wait()

    return pl.pallas_call(
        body,
        out_shape=jax.ShapeDtypeStruct((height, width), F32),
        in_specs=[VMEM] * 8 + [ANY],
        out_specs=ANY,
        scratch_shapes=[pltpu.VMEM((2, strip, width), F32), pltpu.SemaphoreType.DMA((2,))],
        input_output_aliases={8: 0},
        name="finish",
        compiler_params=LEAN,
    )(*near(*prepared, *gots), out)


def local(vectors, reflectors, tfactors, plan):
    groups, strip = plan.shape[0], reflectors.shape[2]
    rows, columns = lax.axis_size("row"), lax.axis_size("col")

    def around(block, shift):
        return lax.ppermute(block, "col", [(c, (c + shift) % columns) for c in range(columns)])

    def trade(block, odd_round):
        route = []
        for row in range(rows):
            for col in range(columns):
                there = row + 1 if (row % 2 == 1) == odd_round else row - 1
                there = (there, col) if 0 <= there < rows else (row, (col + 1) % columns)
                route.append((row * columns + col, there[0] * columns + there[1]))
        return lax.ppermute(block, ("row", "col"), route)

    def everyone(piece, sent):
        return [piece, *(around(sent, shift) for shift in range(1, columns))]

    factors = everyone(tfactors, tfactors)
    plan = plan.reshape(1, groups)
    mark = entry(plan, tfactors)
    later, mark = lax.optimization_barrier((reflectors, mark))
    refls = everyone(reflectors, later)
    mark = entry(vectors, reflectors, after=(mark,))
    kinds, end = tables(mark, tfactors, plan, columns)
    behind = lax.ppermute(end, "row", [(r, (r + 1) % rows) for r in range(rows)])
    current, behinds = vectors, None
    for step in range(0, groups, 2):
        coeffs, projs, gots = [], [], []
        for odd_round in (False, True):
            coeff, proj = edge(current, refls, factors, kinds, step, odd_round)
            coeffs.append(coeff)
            projs.append(proj)
            gots.append(trade(proj, odd_round))
        work, *strips = middle(current, refls, factors, kinds, step, coeffs)
        if behinds is None:
            behind, strips[0] = lax.optimization_barrier((behind, strips[0]))
            behinds = everyone(behind, behind)
        out = store(work, strip)
        prepared = prepare(refls, factors, behinds, kinds, step, strips, projs)
        current = finish(out, prepared, gots)
    return current


def solution(mesh):
    return jax.shard_map(
        local,
        mesh=mesh,
        in_specs=(P("row", "col"), P("col", "row", None), P("col", "row", None, None), P()),
        out_specs=P("row", "col"),
        check_vma=False,
    )
```

```python
import jax
import jax.numpy as jnp
from jax import lax
from jax.experimental import pallas as pl
from jax.experimental.pallas import tpu as pltpu
from jax.sharding import PartitionSpec as P


F32 = jnp.float32
BF16 = jnp.bfloat16
LANES = 128
VMEM = pl.BlockSpec(memory_space=pltpu.VMEM)
HBM = pl.BlockSpec(memory_space=pltpu.HBM)
ANY = pl.BlockSpec(memory_space=pl.ANY)
LEAN = pltpu.CompilerParams(vmem_limit_bytes=8 << 20)


def split(a):
    high = a.astype(BF16)
    return high, (a - high.astype(F32)).astype(BF16)


def dot(a, b, over):
    return lax.dot_general(a, b, (((over,), (0,)), ((), ())), preferred_element_type=F32)


def product(a, b, over=1):
    (ah, al), (bh, bl) = a, b
    if ah.shape[over] > LANES:
        both = dot(jnp.concatenate([ah, al], 1 - over), bh, over)
        rows = ah.shape[1 - over]
        return both[:rows] + (both[rows:] + dot(ah, bl, over))
    return dot(jnp.concatenate([ah, al], over), jnp.concatenate([bh, bh], 0), over) + dot(ah, bl, over)


def pick(kinds, step, pieces):
    value = pieces[0]
    for at, piece in enumerate(pieces[1:], 1):
        mask = jnp.broadcast_to(kinds[step : step + 1, :], value.shape) == at
        value = jnp.where(mask, piece, value)
    return value


def shape(*dims, dtype=F32):
    return pltpu.VMEM(dims, dtype)


def near(*values, space=pltpu.VMEM):
    return [pltpu.with_memory_space_constraint(value, space) for value in values]


def vmem_call(body, outs, *args):
    return pl.pallas_call(
        body, out_shape=outs, in_specs=[VMEM] * len(args), out_specs=[VMEM] * len(outs), compiler_params=LEAN
    )(*near(*args))


def entry(*arrays, after=()):
    lanes = (8, LANES)

    def body(*refs):
        refs[-1][...] = jnp.zeros(lanes, F32)

    return pl.pallas_call(
        body,
        out_shape=shape(*lanes),
        in_specs=[VMEM] * len(after) + [HBM] * len(arrays),
        out_specs=VMEM,
        name="entry",
        compiler_params=LEAN,
    )(*near(*after), *near(*arrays, space=pltpu.HBM))


def fold(f):
    size = f.shape[1]
    part = size // 4
    lane = lax.broadcasted_iota(jnp.int32, (part, size), 1)
    rows = [f[at * part : (at + 1) * part] for at in range(4)]
    mixed = jnp.where(lane < part, pltpu.roll(rows[3], part, 1), rows[1])
    half = part // 2
    halves = jnp.where(lane[:half] < 2 * part, pltpu.roll(rows[2][:half], 2 * part, 1), rows[2][half:])
    return jnp.concatenate([rows[0], mixed, halves], 0)


def unfold(f):
    size = f.shape[1]
    part = size // 4
    half = part // 2
    lane = lax.broadcasted_iota(jnp.int32, (part, size), 1)
    mixed, halves = f[part : 2 * part], f[2 * part :]
    second = jnp.where(lane < part, 0.0, mixed)
    fourth = jnp.where(lane < 3 * part, 0.0, pltpu.roll(mixed, 3 * part, 1))
    third = [jnp.where(lane[:half] < 2 * part, 0.0, v) for v in (pltpu.roll(halves, 2 * part, 1), halves)]
    return jnp.concatenate([f[:part], second, *third, fourth], 0)


def tables(mark, tfactors, plan, columns):
    held, count, lanes = tfactors.shape[:3]
    groups = plan.shape[1]

    def body(_, plan_ref, f_ref, kinds_ref, end_ref):
        for slot in range(held):
            end_ref[slot] = fold(f_ref[slot, count - 1])
        me = lax.axis_index("col")
        kinds_ref[...] = jnp.zeros_like(kinds_ref)
        for step in range(groups):
            group = jnp.broadcast_to(plan_ref[:, step : step + 1], (1, lanes))
            home = group // held if held > 1 else group
            gap = me - home
            gap = jnp.where(gap < 0, gap + columns, gap)
            kinds_ref[step : step + 1, :] = gap * held + (group - home * held)

    table = shape(-(-groups // 8) * 8, lanes, dtype=jnp.int32)
    folded = shape(held, 5 * lanes // 8, lanes)
    return vmem_call(body, [table, folded], mark, plan, tfactors)


def is_top(odd_round):
    return (lax.axis_index("row") % 2 == 1) != odd_round


def ordered(top, low):
    first = is_top(False)
    return jnp.where(first, top, low), jnp.where(first, low, top)


def apart(pieces):
    return [piece.at[slot] for piece in pieces for slot in range(piece.shape[0])]


def edge(x, refls, factors, kinds, step, odd_round):
    width, strip = x.shape[1], refls[0].shape[2]
    block = 2 * strip
    count = factors[0].shape[1]
    n = len(refls)

    def body(kinds_ref, x_ref, *refs):
        refl_refs, factor_refs = apart(refs[:n]), apart(refs[n : 2 * n])
        coeff_ref, proj_ref = refs[-2:]

        def work(at, outer):
            start = at * block
            rows, side = slice(start, start + block), slice(start + outer, start + outer + strip)
            first = split(pick(kinds_ref, step, [r[rows, :] for r in refl_refs]))
            second = split(pick(kinds_ref, step + 1, [r[side, :] for r in refl_refs]))
            high, low = split(x_ref[rows, :])
            cross = product(second, [v[outer : outer + strip] for v in first], over=0)
            blank = jnp.zeros((strip, strip), BF16)
            second = [jnp.concatenate([v, blank] if outer == 0 else [blank, v], 0) for v in second]
            all_high = dot(jnp.concatenate([*first, *second], 1), high, 0)
            all_low = dot(jnp.concatenate([first[0], second[0]], 1), low, 0)
            factor = pick(kinds_ref, step, [r[at] for r in factor_refs])
            weight = product(split(cross), split(factor))
            parts = [all_high[i * strip : (i + 1) * strip] for i in range(4)]
            coeff = parts[0] + (parts[1] + all_low[:strip])
            coeff_ref[...] = coeff
            rest = product(split(weight), split(coeff))
            proj_ref[...] = parts[2] + (parts[3] + all_low[strip:]) - rest

        top = is_top(odd_round)
        pl.when(top)(lambda: work(0, 0))
        pl.when(jnp.logical_not(top))(lambda: work(count - 1, strip))

    args = (kinds, x, *refls, *factors)
    return vmem_call(body, [shape(strip, width)] * 2, *args)


def middle(x, refls, factors, kinds, step, coeffs):
    height, width = x.shape
    strip = refls[0].shape[2]
    block = 2 * strip
    count = height // block
    n = len(refls)

    def body(kinds_ref, x_ref, even_coeff, odd_coeff, *refs):
        refl_refs, factor_refs = apart(refs[:n]), apart(refs[n : 2 * n])
        work_ref, top_ref, low_ref, coeff_ref = refs[2 * n :]
        coeff_ref[0], coeff_ref[count - 1] = ordered(even_coeff[...], odd_coeff[...])

        def run(step, source, blocks, offset, known):
            def rows(at):
                return slice(at * block + offset, (at + 1) * block + offset)

            def refl(at):
                return split(pick(kinds_ref, step, [r[rows(at), :] for r in refl_refs]))

            for at in blocks:
                if at not in known:
                    coeff_ref[at] = product(refl(at), split(source[rows(at), :]), over=0)
            for at in blocks:
                factor = split(pick(kinds_ref, step, [r[at] for r in factor_refs]))
                coeff_ref[at] = product(factor, split(coeff_ref[at]))
            for at in blocks:
                change = product(refl(at), split(coeff_ref[at]))
                work_ref[rows(at), :] = source[rows(at), :] - change

        run(step, x_ref, range(count), 0, (0, count - 1))
        top_ref[...] = work_ref[:strip, :]
        low_ref[...] = work_ref[height - strip :, :]
        run(step + 1, work_ref, range(count - 1), strip, ())

    args = near(kinds, x, *coeffs, *refls, *factors)
    return pl.pallas_call(
        body,
        out_shape=[shape(height, width)] + [shape(strip, width)] * 2,
        in_specs=[VMEM] * len(args),
        out_specs=[VMEM] * 3,
        scratch_shapes=[pltpu.VMEM((count, strip, width), F32)],
        name="middle",
        compiler_params=LEAN,
    )(*args)


def store(work, strip):
    height, width = work.shape

    def body(work_ref, out_ref, sem):
        inner = pl.ds(strip, height - 2 * strip)
        copy = pltpu.make_async_copy(work_ref.at[inner, :], out_ref.at[inner, :], sem)
        copy.start()
        copy.wait()

    return pl.pallas_call(
        body,
        out_shape=jax.ShapeDtypeStruct((height, width), F32),
        in_specs=[VMEM],
        out_specs=ANY,
        scratch_shapes=[pltpu.SemaphoreType.DMA],
        name="store",
        compiler_params=LEAN,
    )(*near(work))


def prepare(refls, factors, behind, kinds, step, strips, projs):
    strip, width = strips[0].shape
    height, count = refls[0].shape[1], factors[0].shape[1]
    n = len(refls)

    def body(kinds_ref, top_ref, low_ref, even_ref, odd_ref, *refs):
        refl_refs, factor_refs = apart(refs[:n]), apart(refs[n : 2 * n])
        behind_refs, refs = apart(refs[2 * n : 3 * n]), refs[3 * n :]
        rests, highs, lows = refs[:2], refs[2:4], refs[4:]
        row, last = lax.axis_index("row"), lax.axis_size("row") - 1
        projs = ordered(even_ref[...], odd_ref[...])

        def weight(start, factor, present):
            refl = pick(kinds_ref, step + 1, [r[start : start + strip, :] for r in refl_refs])
            value = product(split(refl), split(factor))
            return jnp.where(present, value, jnp.zeros_like(value))

        before = unfold(pick(kinds_ref, step + 1, [r[...] for r in behind_refs]))
        own = pick(kinds_ref, step + 1, [r[count - 1] for r in factor_refs])
        top = weight(0, before, row > 0)
        low = weight(height - strip, own, row < last)
        even, odd = ordered(top, low)
        highs[0][...], lows[0][...] = split(even)
        highs[1][...], lows[1][...] = split(odd)
        top = top_ref[...] - product(split(top), split(projs[0]))
        low = low_ref[...] - product(split(low), split(projs[1]))
        rests[0][...], rests[1][...] = ordered(top, low)

    rest, half = shape(strip, width), shape(strip, strip, dtype=BF16)
    return vmem_call(body, [rest, rest, half, half, half, half], *(kinds, *strips, *projs, *refls, *factors, *behind))


def settled(odd_round, rest, high, low, got):
    row, last = lax.axis_index("row"), lax.axis_size("row") - 1
    present = jnp.where(is_top(odd_round), row > 0, row < last)
    other = jnp.where(present, got[...], jnp.zeros_like(got))
    return rest[...] - product((high[...], low[...]), split(other))


def settle(rest, high, low, got):
    def body(*refs):
        refs[-1][...] = settled(False, *refs[:-1])

    return vmem_call(body, [shape(*rest.shape)], rest, high, low, got)[0]


def finish(out, even, rest, high, low, got):
    height, width = out.shape
    strip = rest.shape[0]

    def body(even_ref, *refs):
        out_ref, new_ref, sem = refs[5:]

        def write(odd_round, source):
            start = pl.multiple_of(jnp.where(is_top(odd_round), 0, height - strip), strip)
            rows = out_ref.at[pl.ds(start, strip), :]
            copy = pltpu.make_async_copy(source, rows, sem.at[int(odd_round)])
            copy.start()
            return copy

        first = write(False, even_ref)
        new_ref[...] = settled(True, *refs[:4])
        second = write(True, new_ref)
        first.wait()
        second.wait()

    return pl.pallas_call(
        body,
        out_shape=jax.ShapeDtypeStruct((height, width), F32),
        in_specs=[VMEM] * 5 + [ANY],
        out_specs=ANY,
        scratch_shapes=[pltpu.VMEM((strip, width), F32), pltpu.SemaphoreType.DMA((2,))],
        input_output_aliases={5: 0},
        name="finish",
        compiler_params=LEAN,
    )(*near(even, rest, high, low, got), out)


def local(vectors, reflectors, tfactors, plan):
    groups, strip = plan.shape[0], reflectors.shape[2]
    rows, columns = lax.axis_size("row"), lax.axis_size("col")

    def around(block, shift):
        return lax.ppermute(block, "col", [(c, (c + shift) % columns) for c in range(columns)])

    def trade(block, odd_round):
        route = []
        for row in range(rows):
            for col in range(columns):
                there = row + 1 if (row % 2 == 1) == odd_round else row - 1
                there = (there, col) if 0 <= there < rows else (row, (col + 1) % columns)
                route.append((row * columns + col, there[0] * columns + there[1]))
        return lax.ppermute(block, ("row", "col"), route)

    def everyone(piece, sent):
        return [piece, *(around(sent, shift) for shift in range(1, columns))]

    factors = everyone(tfactors, tfactors)
    plan = plan.reshape(1, groups)
    mark = entry(plan, tfactors)
    later, mark = lax.optimization_barrier((reflectors, mark))
    refls = everyone(reflectors, later)
    mark = entry(vectors, reflectors, after=(mark,))
    kinds, end = tables(mark, tfactors, plan, columns)
    behind = lax.ppermute(end, "row", [(r, (r + 1) % rows) for r in range(rows)])
    current, behinds = vectors, None
    for step in range(0, groups, 2):
        coeffs, projs, gots = [], [], []
        for odd_round in (False, True):
            coeff, proj = edge(current, refls, factors, kinds, step, odd_round)
            coeffs.append(coeff)
            projs.append(proj)
            gots.append(trade(proj, odd_round))
        work, *strips = middle(current, refls, factors, kinds, step, coeffs)
        if behinds is None:
            behind, strips[0] = lax.optimization_barrier((behind, strips[0]))
            behinds = everyone(behind, behind)
        out = store(work, strip)
        prepared = prepare(refls, factors, behinds, kinds, step, strips, projs)
        even = settle(*prepared[::2], gots[0])
        current = finish(out, even, *prepared[1::2], gots[1])
    return current


def solution(mesh):
    return jax.shard_map(
        local,
        mesh=mesh,
        in_specs=(P("row", "col"), P("col", "row", None), P("col", "row", None, None), P()),
        out_specs=P("row", "col"),
        check_vma=False,
    )
```

```python
import jax
import jax.numpy as jnp
from jax import lax
from jax.experimental import pallas as pl
from jax.experimental.pallas import tpu as pltpu
from jax.sharding import PartitionSpec as P


F32 = jnp.float32
BF16 = jnp.bfloat16
LANES = 128
VMEM = pl.BlockSpec(memory_space=pltpu.VMEM)
HBM = pl.BlockSpec(memory_space=pltpu.HBM)
ANY = pl.BlockSpec(memory_space=pl.ANY)
LEAN = pltpu.CompilerParams(vmem_limit_bytes=8 << 20)


def split(a):
    high = a.astype(BF16)
    return high, (a - high.astype(F32)).astype(BF16)


def dot(a, b, over):
    return lax.dot_general(a, b, (((over,), (0,)), ((), ())), preferred_element_type=F32)


def product(a, b, over=1):
    (ah, al), (bh, bl) = a, b
    if ah.shape[over] > LANES:
        both = dot(jnp.concatenate([ah, al], 1 - over), bh, over)
        rows = ah.shape[1 - over]
        return both[:rows] + (both[rows:] + dot(ah, bl, over))
    return dot(jnp.concatenate([ah, al], over), jnp.concatenate([bh, bh], 0), over) + dot(ah, bl, over)


def pick(kinds, step, pieces):
    value = pieces[0]
    for at, piece in enumerate(pieces[1:], 1):
        mask = jnp.broadcast_to(kinds[step : step + 1, :], value.shape) == at
        value = jnp.where(mask, piece, value)
    return value


def shape(*dims, dtype=F32):
    return pltpu.VMEM(dims, dtype)


def near(*values, space=pltpu.VMEM):
    return [pltpu.with_memory_space_constraint(value, space) for value in values]


def vmem_call(body, outs, *args):
    return pl.pallas_call(
        body, out_shape=outs, in_specs=[VMEM] * len(args), out_specs=[VMEM] * len(outs), compiler_params=LEAN
    )(*near(*args))


def entry(*arrays, after=()):
    lanes = (8, LANES)

    def body(*refs):
        refs[-1][...] = jnp.zeros(lanes, F32)

    return pl.pallas_call(
        body,
        out_shape=shape(*lanes),
        in_specs=[VMEM] * len(after) + [HBM] * len(arrays),
        out_specs=VMEM,
        name="entry",
        compiler_params=LEAN,
    )(*near(*after), *near(*arrays, space=pltpu.HBM))


def fold(f):
    size = f.shape[1]
    part = size // 4
    lane = lax.broadcasted_iota(jnp.int32, (part, size), 1)
    rows = [f[at * part : (at + 1) * part] for at in range(4)]
    mixed = jnp.where(lane < part, pltpu.roll(rows[3], part, 1), rows[1])
    half = part // 2
    halves = jnp.where(lane[:half] < 2 * part, pltpu.roll(rows[2][:half], 2 * part, 1), rows[2][half:])
    return jnp.concatenate([rows[0], mixed, halves], 0)


def unfold(f):
    size = f.shape[1]
    part = size // 4
    half = part // 2
    lane = lax.broadcasted_iota(jnp.int32, (part, size), 1)
    mixed, halves = f[part : 2 * part], f[2 * part :]
    second = jnp.where(lane < part, 0.0, mixed)
    fourth = jnp.where(lane < 3 * part, 0.0, pltpu.roll(mixed, 3 * part, 1))
    third = [jnp.where(lane[:half] < 2 * part, 0.0, v) for v in (pltpu.roll(halves, 2 * part, 1), halves)]
    return jnp.concatenate([f[:part], second, *third, fourth], 0)


def tables(mark, tfactors, plan, columns):
    held, count, lanes = tfactors.shape[:3]
    groups = plan.shape[1]

    def body(_, plan_ref, f_ref, kinds_ref, end_ref):
        for slot in range(held):
            end_ref[slot] = fold(f_ref[slot, count - 1])
        me = lax.axis_index("col")
        kinds_ref[...] = jnp.zeros_like(kinds_ref)
        for step in range(groups):
            group = jnp.broadcast_to(plan_ref[:, step : step + 1], (1, lanes))
            home = group // held if held > 1 else group
            gap = me - home
            gap = jnp.where(gap < 0, gap + columns, gap)
            kinds_ref[step : step + 1, :] = gap * held + (group - home * held)

    table = shape(-(-groups // 8) * 8, lanes, dtype=jnp.int32)
    folded = shape(held, 5 * lanes // 8, lanes)
    return vmem_call(body, [table, folded], mark, plan, tfactors)


def is_top(odd_round):
    return (lax.axis_index("row") % 2 == 1) != odd_round


def ordered(top, low):
    first = is_top(False)
    return jnp.where(first, top, low), jnp.where(first, low, top)


def apart(pieces):
    return [piece.at[slot] for piece in pieces for slot in range(piece.shape[0])]


def edge(x, refls, factors, kinds, step, odd_round):
    width, strip = x.shape[1], refls[0].shape[2]
    block = 2 * strip
    count = factors[0].shape[1]
    n = len(refls)

    def body(kinds_ref, x_ref, *refs):
        refl_refs, factor_refs = apart(refs[:n]), apart(refs[n : 2 * n])
        coeff_ref, proj_ref = refs[-2:]

        def work(at, outer):
            start = at * block
            rows, side = slice(start, start + block), slice(start + outer, start + outer + strip)
            first = split(pick(kinds_ref, step, [r[rows, :] for r in refl_refs]))
            second = split(pick(kinds_ref, step + 1, [r[side, :] for r in refl_refs]))
            high, low = split(x_ref[rows, :])
            cross = product(second, [v[outer : outer + strip] for v in first], over=0)
            blank = jnp.zeros((strip, strip), BF16)
            second = [jnp.concatenate([v, blank] if outer == 0 else [blank, v], 0) for v in second]
            all_high = dot(jnp.concatenate([*first, *second], 1), high, 0)
            all_low = dot(jnp.concatenate([first[0], second[0]], 1), low, 0)
            factor = pick(kinds_ref, step, [r[at] for r in factor_refs])
            weight = product(split(cross), split(factor))
            parts = [all_high[i * strip : (i + 1) * strip] for i in range(4)]
            coeff = parts[0] + (parts[1] + all_low[:strip])
            coeff_ref[...] = coeff
            rest = product(split(weight), split(coeff))
            proj_ref[...] = parts[2] + (parts[3] + all_low[strip:]) - rest

        top = is_top(odd_round)
        pl.when(top)(lambda: work(0, 0))
        pl.when(jnp.logical_not(top))(lambda: work(count - 1, strip))

    args = (kinds, x, *refls, *factors)
    return vmem_call(body, [shape(strip, width)] * 2, *args)


def middle(x, refls, factors, kinds, step, coeffs):
    height, width = x.shape
    strip = refls[0].shape[2]
    block = 2 * strip
    count = height // block
    n = len(refls)

    def body(kinds_ref, x_ref, even_coeff, odd_coeff, *refs):
        refl_refs, factor_refs = apart(refs[:n]), apart(refs[n : 2 * n])
        work_ref, top_ref, low_ref, coeff_ref = refs[2 * n :]
        coeff_ref[0], coeff_ref[count - 1] = ordered(even_coeff[...], odd_coeff[...])

        def run(step, source, blocks, offset, known):
            def rows(at):
                return slice(at * block + offset, (at + 1) * block + offset)

            def refl(at):
                return split(pick(kinds_ref, step, [r[rows(at), :] for r in refl_refs]))

            for at in blocks:
                if at not in known:
                    coeff_ref[at] = product(refl(at), split(source[rows(at), :]), over=0)
            for at in blocks:
                factor = split(pick(kinds_ref, step, [r[at] for r in factor_refs]))
                coeff_ref[at] = product(factor, split(coeff_ref[at]))
            for at in blocks:
                change = product(refl(at), split(coeff_ref[at]))
                work_ref[rows(at), :] = source[rows(at), :] - change

        run(step, x_ref, range(count), 0, (0, count - 1))
        top_ref[...] = work_ref[:strip, :]
        low_ref[...] = work_ref[height - strip :, :]
        run(step + 1, work_ref, range(count - 1), strip, ())

    args = near(kinds, x, *coeffs, *refls, *factors)
    return pl.pallas_call(
        body,
        out_shape=[shape(height, width)] + [shape(strip, width)] * 2,
        in_specs=[VMEM] * len(args),
        out_specs=[VMEM] * 3,
        scratch_shapes=[pltpu.VMEM((count, strip, width), F32)],
        name="middle",
        compiler_params=LEAN,
    )(*args)


def store(work, strip):
    height, width = work.shape

    def body(work_ref, out_ref, sem):
        inner = pl.ds(strip, height - 2 * strip)
        copy = pltpu.make_async_copy(work_ref.at[inner, :], out_ref.at[inner, :], sem)
        copy.start()
        copy.wait()

    return pl.pallas_call(
        body,
        out_shape=jax.ShapeDtypeStruct((height, width), F32),
        in_specs=[VMEM],
        out_specs=ANY,
        scratch_shapes=[pltpu.SemaphoreType.DMA],
        name="store",
        compiler_params=LEAN,
    )(*near(work))


def prepare(refls, factors, behind, kinds, step, strips, projs):
    strip, width = strips[0].shape
    height, count = refls[0].shape[1], factors[0].shape[1]
    n = len(refls)

    def body(kinds_ref, top_ref, low_ref, even_ref, odd_ref, *refs):
        refl_refs, factor_refs = apart(refs[:n]), apart(refs[n : 2 * n])
        behind_refs, refs = apart(refs[2 * n : 3 * n]), refs[3 * n :]
        rests, highs, lows = refs[:2], refs[2:4], refs[4:]
        row, last = lax.axis_index("row"), lax.axis_size("row") - 1
        projs = ordered(even_ref[...], odd_ref[...])

        def weight(start, factor, present):
            refl = pick(kinds_ref, step + 1, [r[start : start + strip, :] for r in refl_refs])
            value = product(split(refl), split(factor))
            return jnp.where(present, value, jnp.zeros_like(value))

        before = unfold(pick(kinds_ref, step + 1, [r[...] for r in behind_refs]))
        own = pick(kinds_ref, step + 1, [r[count - 1] for r in factor_refs])
        top = weight(0, before, row > 0)
        low = weight(height - strip, own, row < last)
        even, odd = ordered(top, low)
        highs[0][...], lows[0][...] = split(even)
        highs[1][...], lows[1][...] = split(odd)
        top = top_ref[...] - product(split(top), split(projs[0]))
        low = low_ref[...] - product(split(low), split(projs[1]))
        rests[0][...], rests[1][...] = ordered(top, low)

    rest, half = shape(strip, width), shape(strip, strip, dtype=BF16)
    return vmem_call(body, [rest, rest, half, half, half, half], *(kinds, *strips, *projs, *refls, *factors, *behind))


def settled(odd_round, rest, high, low, got):
    row, last = lax.axis_index("row"), lax.axis_size("row") - 1
    present = jnp.where(is_top(odd_round), row > 0, row < last)
    other = jnp.where(present, got[...], jnp.zeros_like(got))
    return rest[...] - product((high[...], low[...]), split(other))


def settle(rest, high, low, got):
    def body(*refs):
        refs[-1][...] = settled(False, *refs[:-1])

    return vmem_call(body, [shape(*rest.shape)], rest, high, low, got)[0]


def finish(out, even, rest, high, low, got):
    height, width = out.shape
    strip = rest.shape[0]

    def body(even_ref, *refs):
        out_ref, new_ref, sem = refs[5:]

        def write(odd_round, source, lanes, at):
            start = pl.multiple_of(jnp.where(is_top(odd_round), 0, height - strip), strip)
            rows = out_ref.at[pl.ds(start, strip), lanes]
            copy = pltpu.make_async_copy(source.at[:, lanes], rows, sem.at[at])
            copy.start()
            return copy

        copies = [write(False, even_ref, pl.ds(0, width), 0)]
        for at in range(width // LANES):
            lanes = pl.ds(at * LANES, LANES)
            got_ref = refs[3].at[:, lanes]
            new_ref[:, lanes] = settled(True, refs[0].at[:, lanes], *refs[1:3], got_ref)
            copies.append(write(True, new_ref, lanes, at + 1))
        for copy in copies:
            copy.wait()

    return pl.pallas_call(
        body,
        out_shape=jax.ShapeDtypeStruct((height, width), F32),
        in_specs=[VMEM] * 5 + [ANY],
        out_specs=ANY,
        scratch_shapes=[
            pltpu.VMEM((strip, width), F32),
            pltpu.SemaphoreType.DMA((1 + width // LANES,)),
        ],
        input_output_aliases={5: 0},
        name="finish",
        compiler_params=LEAN,
    )(*near(even, rest, high, low, got), out)


def local(vectors, reflectors, tfactors, plan):
    groups, strip = plan.shape[0], reflectors.shape[2]
    rows, columns = lax.axis_size("row"), lax.axis_size("col")

    def around(block, shift):
        return lax.ppermute(block, "col", [(c, (c + shift) % columns) for c in range(columns)])

    def trade(block, odd_round):
        route = []
        for row in range(rows):
            for col in range(columns):
                there = row + 1 if (row % 2 == 1) == odd_round else row - 1
                there = (there, col) if 0 <= there < rows else (row, (col + 1) % columns)
                route.append((row * columns + col, there[0] * columns + there[1]))
        return lax.ppermute(block, ("row", "col"), route)

    def everyone(piece, sent):
        return [piece, *(around(sent, shift) for shift in range(1, columns))]

    factors = everyone(tfactors, tfactors)
    plan = plan.reshape(1, groups)
    mark = entry(plan, tfactors)
    later, mark = lax.optimization_barrier((reflectors, mark))
    refls = everyone(reflectors, later)
    mark = entry(vectors, reflectors, after=(mark,))
    kinds, end = tables(mark, tfactors, plan, columns)
    behind = lax.ppermute(end, "row", [(r, (r + 1) % rows) for r in range(rows)])
    current, behinds = vectors, None
    for step in range(0, groups, 2):
        coeffs, projs, gots = [], [], []
        for odd_round in (False, True):
            coeff, proj = edge(current, refls, factors, kinds, step, odd_round)
            coeffs.append(coeff)
            projs.append(proj)
            gots.append(trade(proj, odd_round))
        work, *strips = middle(current, refls, factors, kinds, step, coeffs)
        if behinds is None:
            behind, strips[0] = lax.optimization_barrier((behind, strips[0]))
            behinds = everyone(behind, behind)
        out = store(work, strip)
        prepared = prepare(refls, factors, behinds, kinds, step, strips, projs)
        even = settle(*prepared[::2], gots[0])
        current = finish(out, even, *prepared[1::2], gots[1])
    return current


def solution(mesh):
    return jax.shard_map(
        local,
        mesh=mesh,
        in_specs=(P("row", "col"), P("col", "row", None), P("col", "row", None, None), P()),
        out_specs=P("row", "col"),
        check_vma=False,
    )
```
